256 devices in a mesh: tok: 32 (over y, z), head: 8 (over x, core).
Axes of the slice: x: 4, y: 4, z: 8, core: 2. Of those that a mesh axis runs over, the one named last changes fastest.
Arguments:
- guess: float32 [4096, 1024], P('tok', 'head'), may hold values from -4 to 4
- drive: float32 [4096, 1024], P('tok', 'head'), may hold values from -2 to 2
- decay: float32 [4096, 1024], P('tok', 'head'), may hold values from 0 to 1
- mixing: float32 [1024], P('head'), may hold values from 0.1 to 0.5
- init_state: float32 [1024], P('head'), may hold values from -6 to 6
- skew_gen: float32 [8, 128, 128], P('head'), as said below
- w_up: bfloat16 [1024, 4096], P(None, 'head'), may hold values from -0.1875 to 0.1875
- w_down: bfloat16 [1024, 4096], P(None, 'head'), may hold values from -0.09375 to 0.09375
- cotangent: bfloat16 [4096, 1024], P('tok', 'head'), may hold values from -6 to 6
Outputs:
- states: float32 [4096, 1024], P('tok', 'head')
- mlp_out: bfloat16 [4096, 1024], P('tok', 'head')
- state_grad: bfloat16 [4096, 1024], P('tok', 'head')
- grad_up: float32 [1024, 4096], P('tok', 'head')
- grad_down: float32 [1024, 4096], P('tok', 'head')
The draws below stay inside these ranges and needn't reach their ends.
Inputs may be any that keep to these rules, and one draw needn't show every extreme that they name: `skew_gen`: each head's matrix is skew-symmetric.
All inputs are finite; a program needn't handle non-finite values.
Results may differ from the reference program's by a relative error of at most 0.017.
Values may be sent and summed in bfloat16 or wider, within the bound.
A program may use at most 64 MiB of HBM per device.

```python
import math
import jax
import jax.numpy as jnp
from jax import lax

STATE = 128
FF = 4096
TOK_DEV = 128
HEADS = 8
D = 1024
SEQUENCE_TOKENS = 4096


def head_classes(key):
    order = jax.random.permutation(jax.random.fold_in(key, 101), HEADS)
    return order >= HEADS // 2


def per_channel(values):
    return jnp.repeat(values, STATE, axis=-1)


def head_noise(key, shape):
    return jnp.clip(jax.random.normal(key, shape, jnp.float32), -5.0, 5.0)


def draw_guess(key, part):
    lasting = head_classes(key)
    key_scale, key_noise = jax.random.split(jax.random.fold_in(key, 303))
    quick_scale = jax.random.uniform(key_scale, (HEADS,), jnp.float32, 0.3, 0.7)
    scales = jnp.where(lasting, 0.2 / math.sqrt(SEQUENCE_TOKENS), quick_scale)
    return head_noise(key_noise, (SEQUENCE_TOKENS, D)) * per_channel(scales)[None, :]


def draw_drive(key, part):
    lasting = head_classes(key)
    key_noise = jax.random.fold_in(key, 404)
    scales = jnp.where(lasting, 1.5 / math.sqrt(SEQUENCE_TOKENS), 0.3)
    return head_noise(key_noise, (SEQUENCE_TOKENS, D)) * per_channel(scales)[None, :]


def draw_decay(key, part):
    lasting = head_classes(key)
    key_slow, random_seed_fast, key_group, key_rough, key_spots = jax.random.split(jax.random.fold_in(key, 202), 5)
    slow_rate = 1.0 / (SEQUENCE_TOKENS * jnp.exp(jax.random.uniform(key_slow, (HEADS,), jnp.float32, math.log(2.0), math.log(8.0))))
    rapid_fraction = jnp.exp(jax.random.uniform(random_seed_fast, (HEADS,), jnp.float32, math.log(0.005), math.log(0.03)))
    attention_decay_speed = jnp.where(lasting, slow_rate, rapid_fraction)
    group_factor = jax.random.uniform(key_group, (SEQUENCE_TOKENS // TOK_DEV, HEADS), jnp.float32, 0.5, 1.5)
    roughness = jax.random.uniform(key_rough, (SEQUENCE_TOKENS, D), jnp.float32, 0.5, 1.5)
    decay_speeds = jnp.repeat(per_channel(attention_decay_speed[None, :] * group_factor), TOK_DEV, axis=0) * roughness
    kept_entry_selector = jnp.exp(-decay_speeds)
    flagged_spots = jax.random.randint(key_spots, (3,), 0, SEQUENCE_TOKENS)
    symbol_locations = jnp.arange(SEQUENCE_TOKENS)[:, None]
    vocabulary_groupings = jnp.any(symbol_locations == flagged_spots[None, :], axis=1)
    return jnp.where(vocabulary_groupings[:, None], 0.6 * kept_entry_selector, kept_entry_selector)


def draw_skew_gen(key, part):
    raw_values = jax.random.normal(key, (HEADS, STATE, STATE), jnp.float32) * (0.5 / math.sqrt(STATE))
    return raw_values - jnp.swapaxes(raw_values, 1, 2)


def spiked(values, rng, source, target, shards_of, factor):
    owner, partner = [(jnp.arange(values.shape[axis_at]) // (values.shape[axis_at] // shards_of)).reshape([-1 if axis == axis_at else 1 for axis in range(values.ndim)]) for axis_at in (source, target)]
    chosen = jax.random.permutation(rng, shards_of)[partner]
    strong = (owner == chosen) | (owner == (partner + shards_of // 2) % shards_of)
    return jnp.where(strong, factor * values, values)


def steps_of(key, dims, cuts, least, largest):
    def one(dim, shards_of):
        steps = jax.random.uniform(jax.random.fold_in(jax.random.fold_in(key, 6), dim), (shards_of,), jnp.float32, least / len(cuts), largest / len(cuts))
        return jnp.repeat(jnp.exp(steps), dims[dim] // shards_of).reshape((-1,) + (1,) * (len(dims) - dim - 1))

    gain = one(*cuts[0])
    for cut in cuts[1:]:
        gain = gain * one(*cut)
    return gain


def centred(key, shape, spread, most, cuts=(), held_as=jnp.bfloat16):
    level = steps_of(key, shape, cuts, -0.22, 0.18) if cuts else 1.0
    result = jax.random.normal(key, shape, jnp.float32) * spread * level
    return jnp.minimum(jnp.maximum(result, -most), most).astype(held_as)


def heavy_noise(key, shape, scale, bound, pieces, heavy, kind=jnp.bfloat16):
    result = scale * jax.random.normal(key, shape, jnp.float32)
    if pieces:
        result = result * steps_of(key, shape, pieces, -0.22, 0.18)
    return jnp.clip(spiked(result, jax.random.fold_in(key, 3), *heavy), -bound, bound).astype(kind)


def setup_inputs(seed: int = 0) -> dict:
    splits = jax.random.split(jax.random.key(seed), 10)
    return {
        "guess": draw_guess(jax.random.fold_in(splits[9], 71), 0),
        "drive": draw_drive(jax.random.fold_in(splits[9], 71), 0),
        "decay": draw_decay(jax.random.fold_in(splits[9], 71), 0),
        "mixing": jnp.clip(0.1 + 0.4 * jax.random.uniform(splits[3], (D,), jnp.float32) ** steps_of(splits[3], (D,), ((0, 8),), -0.2, 0.2), 0.1, 0.5),
        "init_state": centred(splits[4], (D,), 1.0, 6.0, ((0, 8),), jnp.float32),
        "skew_gen": draw_skew_gen(jax.random.fold_in(splits[9], 71), 0),
        "w_up": centred(splits[6], (D, FF), D ** -0.5, 0.1875, ((1, 8),)),
        "w_down": centred(splits[7], (D, FF), FF ** -0.5, 0.09375, ((1, 8),)),
        "cotangent": heavy_noise(splits[8], (SEQUENCE_TOKENS, D), 1.0, 6.0, ((0, 32), (1, 8)), (0, 1, 32, 2.75)),
    }


exact_precision = lax.Precision.HIGHEST

def cayley(antisymmetric_matrix):
    identity = jnp.eye(antisymmetric_matrix.shape[0], dtype=jnp.float32)
    raised = identity + antisymmetric_matrix
    shifted = identity - jnp.dot(antisymmetric_matrix, antisymmetric_matrix, precision=exact_precision)
    factor = jnp.linalg.cholesky(shifted)
    squared = jnp.dot(raised, raised, precision=exact_precision)
    return jax.scipy.linalg.cho_solve((factor, True), squared.T).T

def tangent_approximate(before, decay, mixing):
    bent_values = jnp.tanh(before)
    curvature = 1.0 - bent_values * bent_values
    gradient_inclines = (1.0 - mixing) * decay + mixing * curvature
    pushes = mixing * (bent_values - curvature * before)
    return (gradient_inclines, pushes)

def reference(guess, drive, decay, mixing, init_state, skew_gen, w_up, w_down, cotangent):
    rotations = jax.vmap(cayley)(skew_gen)
    tokens_all = guess.shape[0]
    before = jnp.concatenate([init_state[None, :], guess[:-1]], axis=0)
    gradient_inclines, pushes = tangent_approximate(before, decay, mixing[None, :])
    gradient_inclines = gradient_inclines.reshape(tokens_all, HEADS, STATE)
    pushes = pushes.reshape(tokens_all, HEADS, STATE)
    offsets = jnp.einsum('hij,thj->thi', rotations, pushes, precision=exact_precision)
    offsets = offsets + drive.reshape(tokens_all, HEADS, STATE)

    def advance(carried, inputs):
        slope_row, bias_vector_line = inputs
        following = jnp.einsum('hij,hj->hi', rotations, slope_row * carried, precision=exact_precision) + bias_vector_line
        return (following, following)
    final_state, states = lax.scan(advance, init_state.reshape(HEADS, STATE), (gradient_inclines, offsets))
    states = states.reshape(tokens_all, HEADS * STATE)
    features = states.astype(jnp.bfloat16)
    hidden_pre = jnp.dot(features.astype(jnp.float32), w_up.astype(jnp.float32), preferred_element_type=jnp.float32)
    logistic_gate = jax.nn.sigmoid(hidden_pre)
    hidden = (hidden_pre * logistic_gate).astype(jnp.bfloat16)
    mlp_out = lax.dot_general(hidden.astype(jnp.float32), w_down.astype(jnp.float32), (((1,), (1,)), ((), ())), preferred_element_type=jnp.float32).astype(jnp.bfloat16)
    hidden_grad = jnp.dot(cotangent.astype(jnp.float32), w_down.astype(jnp.float32), preferred_element_type=jnp.float32)
    pre_grad = (hidden_grad * logistic_gate * (1.0 + hidden_pre * (1.0 - logistic_gate))).astype(jnp.bfloat16)
    state_grad = lax.dot_general(pre_grad.astype(jnp.float32), w_up.astype(jnp.float32), (((1,), (1,)), ((), ())), preferred_element_type=jnp.float32).astype(jnp.bfloat16)
    grad_up = lax.dot_general(features.astype(jnp.float32), pre_grad.astype(jnp.float32), (((0,), (0,)), ((), ())), preferred_element_type=jnp.float32)
    grad_down = lax.dot_general(cotangent.astype(jnp.float32), hidden.astype(jnp.float32), (((0,), (0,)), ((), ())), preferred_element_type=jnp.float32)
    return (states, mlp_out, state_grad, grad_up, grad_down)
```

```python
import functools

import jax
import jax.numpy as jnp
from jax import lax
from jax.experimental import pallas as pl
from jax.experimental.pallas import tpu as pltpu
from jax.sharding import PartitionSpec as P

MESH = pl.DeviceIdType.MESH
F32, BF16 = jnp.float32, jnp.bfloat16
S = 128
NZ = 8
NB, L = 8, 16
MR = 144
SENT = 136
CUT = 72
NEWTON = 14


def split(x):
    hi = x.astype(BF16)
    return hi, (x - hi.astype(F32)).astype(BF16)


def left(x):
    return jnp.concatenate(split(x), axis=1)


def right(x):
    both = jnp.concatenate(split(x), axis=1)
    return jnp.concatenate([both, both], axis=0)


def product(l, r):
    out = jnp.dot(l, r, preferred_element_type=F32)
    return out[:, :S] + out[:, S:]


def mm(a, b):
    return product(left(a), right(b))


def compose(first, then):
    out = mm(first, then[:S])
    return jnp.concatenate([out[:S], out[S:] + then[S:]], axis=0)


def eye():
    rows = lax.broadcasted_iota(jnp.int32, (S, S), 0)
    cols = lax.broadcasted_iota(jnp.int32, (S, S), 1)
    return jnp.where(rows == cols, 1.0, 0.0).astype(F32)


def column(v, unit):
    return jnp.sum(unit * v, axis=1, keepdims=True)


def apply_map(v, m, unit):
    return jnp.sum(column(v, unit) * m[:S], axis=0, keepdims=True) + m[S : S + 1]


def dot_t(a, b):
    return lax.dot_general(a, b, (((1,), (1,)), ((), ())), preferred_element_type=F32)


class Ring:
    def __init__(self, n, me, device, blocks, landing, send, recv, half):
        self.n, self.me, self.device = n, me, device
        self.blocks, self.landing, self.send, self.recv, self.half = blocks, landing, send, recv, half

    def piece(self, owner, c):
        return self.blocks.at[owner, pl.ds(c * self.half, self.half)]

    def copy(self, d, hop, c):
        way = 1 if d == 0 else -1
        owner = lax.rem(self.me + way * (self.n // 2 - hop) + 2 * self.n, self.n)
        target = lax.rem(self.me + way + self.n, self.n)
        return pltpu.make_async_remote_copy(
            src_ref=self.piece(owner, c),
            dst_ref=self.landing.at[d, hop, c],
            send_sem=self.send.at[d, hop, c],
            recv_sem=self.recv.at[d, hop, c],
            device_id=self.device(target),
            device_id_type=MESH,
        )

    def begin(self):
        for d in range(2):
            self.copy(d, 0, d).start()
        if self.n > 2:
            for d in range(2):
                self.copy(d, 1, 1 - d).start()

    def pieces(self, hop):
        return [(d, c) for c in range(2) for d in range(2) if hop > 0 or c == d]

    def advance(self, hop):
        last = hop == self.n // 2 - 1
        order = [(d, 1 - d) for d in range(2)] + [(d, d) for d in range(2)]
        for d, c in order:
            if hop == 0 and c != d:
                continue
            self.copy(d, hop, c).wait_recv()
            if last:
                continue
            way = 1 if d == 0 else -1
            owner = lax.rem(self.me + way * (self.n // 2 - hop - 1) + 2 * self.n, self.n)
            mine = self.blocks[owner, pl.ds(c * self.half, self.half)]
            came = self.landing[d, hop, c]
            if not (hop == 0 and False):
                self.blocks[owner, pl.ds(c * self.half, self.half)] = (
                    mine.astype(F32) + came.astype(F32)
                ).astype(BF16)
            self.copy(d, hop + 1, c).start()

    def total(self, c):
        last = self.n // 2 - 1
        out = self.blocks[self.me, pl.ds(c * self.half, self.half)].astype(F32)
        for d in range(2):
            if (d, c) in self.pieces(last):
                out = out + self.landing[d, last, c].astype(F32)
        return out

    def finish(self):
        for hop in range(self.n // 2):
            for d, c in self.pieces(hop):
                self.copy(d, hop, c).wait_send()


def kernel(
    ntok,
    nhead,
    guess,
    drive,
    decay,
    mixing,
    init,
    skew,
    w_up_hbm,
    w_down_hbm,
    cot,
    states_out,
    mlp_out,
    sgrad_out,
    gup_out,
    gdown_out,
    w_up,
    w_down,
    w_sem,
    shifted,
    row_send,
    row_recv,
    zinv,
    wrot,
    slopes,
    offs,
    pre_maps,
    shifts,
    bmaps,
    bpre,
    gath,
    gsend,
    grecv,
    table,
    vin,
    vout,
    v_send,
    v_recv,
    feats,
    f_send,
    f_recv,
    cots,
    c_send,
    c_recv,
    hgrad,
    ftrans,
    ctrans,
    parts,
    landed,
    o_send,
    o_recv,
    ublk,
    dblk,
    u2blk,
    d2blk,
    la1,
    la2,
    lb1,
    lb2,
    a1s,
    a1r,
    a2s,
    a2r,
    b1s,
    b1r,
    b2s,
    b2r,
):
    ny, nx = ntok // NZ, nhead // 2
    tok, head = lax.axis_index("tok"), lax.axis_index("head")
    y, z = lax.div(tok, NZ), lax.rem(tok, NZ)
    x, core = lax.div(head, 2), lax.rem(head, 2)

    def along_z(target):
        return {"tok": y * NZ + target, "head": head}

    def along_y(target):
        return {"tok": target * NZ + z, "head": head}

    def at_tok(target):
        return {"tok": target, "head": head}

    def at_head(target):
        return {"tok": tok, "head": target}

    peers = [(dx, flip) for dx in ([0, 1, nx - 1, 2] if nx >= 4 else range(nx)) for flip in (1, 0)]
    peers = [q for q in peers if q != (0, 0)]

    def peer(q):
        return lax.rem(x + q[0], nx) * 2 + lax.rem(core + q[1], 2)

    after, before_me = lax.rem(tok + 1, ntok), lax.rem(tok + ntok - 1, ntok)

    barrier = pltpu.get_barrier_semaphore()
    greet = [along_z(lax.rem(z + 1, NZ)), along_z(lax.rem(z + NZ - 1, NZ))]
    greet += [along_y(lax.rem(y + 1, ny)), along_y(lax.rem(y + ny - 1, ny))]
    greet += [at_tok(after), at_tok(before_me)]
    greet += [at_head(peer(q)) for q in peers]
    for who in greet:
        pl.semaphore_signal(barrier, inc=1, device_id=who, device_id_type=MESH)
    loads = [
        pltpu.make_async_copy(w_up_hbm, w_up, w_sem.at[0]),
        pltpu.make_async_copy(w_down_hbm, w_down, w_sem.at[1]),
    ]
    for load in loads:
        load.start()

    unit = eye()
    k = skew[...]
    a = unit + k
    kk = mm(k, k)
    bound = jnp.sqrt(jnp.sum(jnp.sum(kk * kk, axis=1, keepdims=True), axis=0, keepdims=True) * 0.5)
    top = 1.0 + 1.01 * bound
    zinv[...] = (unit - k) * (2.0 / (1.0 + top))
    gap = (top - 1.0) / (top + 1.0)
    a_left = left(a)

    def newton(_, gap):
        v = zinv[...]
        t = product(a_left, right(v))
        square = gap * gap
        zinv[...] = (2.0 * v - mm(v, t)) * (2.0 / (2.0 - square))
        return square / (2.0 - square)

    gap = lax.fori_loop(0, NEWTON // 2, newton, gap)

    pl.semaphore_wait(barrier, len(greet))
    row_copy = pltpu.make_async_remote_copy(
        src_ref=guess.at[pl.ds(S - 8, 8)],
        dst_ref=shifted.at[pl.ds(0, 8)],
        send_sem=row_send,
        recv_sem=row_recv,
        device_id=at_tok(after),
        device_id_type=MESH,
    )
    row_copy.start()

    def head_copy(q, src, dst, send, recv):
        return pltpu.make_async_remote_copy(
            src_ref=src,
            dst_ref=dst,
            send_sem=send.at[q[0] * 2 + q[1]],
            recv_sem=recv.at[q[0] * 2 + q[1]],
            device_id=at_head(peer(q)),
            device_id_type=MESH,
        )

    def back(q):
        return lax.rem(x + nx - q[0], nx) * 2 + lax.rem(core + q[1], 2)

    for q in peers:
        head_copy(q, cot, cots.at[head], c_send, c_recv).start()
    cots[head] = cot[...]

    lax.fori_loop(NEWTON // 2, NEWTON, newton, gap)
    v = zinv[...]
    t = jnp.dot(a, v, precision=lax.Precision.HIGHEST, preferred_element_type=F32)
    v = v + mm(v, unit - t)
    rot_t = 2.0 * v - unit
    wrot[...] = right(rot_t)

    shifted[pl.ds(8, S), :] = guess[...]
    row_copy.wait_recv()
    before = shifted[pl.ds(7, S), :]
    first = (lax.broadcasted_iota(jnp.int32, (S, S), 0) == 0) & (tok == 0)
    before = jnp.where(first, init[...], before)
    m = mixing[...]
    bent = jnp.tanh(before)
    curve = 1.0 - bent * bent
    slopes[...] = (1.0 - m) * decay[...] + m * curve
    offs[...] = product(left(m * (bent - curve * before)), wrot[...]) + drive[...]

    def advance(step, blocks, shift):
        rows = [left(blocks[b] * slopes[pl.ds(b * L + step, 1), :]) for b in range(NB)]
        shift = shift * slopes[pl.ds(step, NB, stride=L), :]
        rows.append(left(jnp.concatenate([shift, jnp.zeros((16 - NB, S), F32)], axis=0)))
        out = product(jnp.concatenate(rows, axis=0), wrot[...])
        for b in range(NB):
            pre_maps[b * L + step] = out[b * S : (b + 1) * S]
        shifts[step] = out[NB * S : NB * S + NB] + offs[pl.ds(step, NB, stride=L), :]

    advance(0, [unit] * NB, jnp.zeros((NB, S), F32))

    def later(step, _):
        advance(step, [pre_maps[b * L + step - 1] for b in range(NB)], shifts[step - 1])
        return 0

    lax.fori_loop(1, L, later, 0)

    pad = jnp.zeros((MR - S - 1, S), F32)

    def block_map(b):
        return jnp.concatenate([pre_maps[b * L + L - 1], shifts[L - 1, b : b + 1], pad], axis=0)

    none = jnp.concatenate([unit, jnp.zeros((MR - S, S), F32)], axis=0)
    bpre[0] = none
    bpre[1] = block_map(0)
    bpre[2] = compose(block_map(0), block_map(1))
    bmaps[0] = compose(block_map(2), block_map(3))
    bmaps[1] = compose(block_map(4), block_map(5))
    bmaps[2] = compose(block_map(6), block_map(7))
    bpre[4] = compose(bpre[2], bmaps[0])
    bmaps[3] = compose(bmaps[1], bmaps[2])
    gath[z] = compose(bpre[4], bmaps[3])

    cuts = ((0, CUT), (CUT, SENT - CUT))

    def hop(d, k, c):
        way = 1 if d == 0 else -1
        part = gath.at[lax.rem(z - way * k + 2 * NZ, NZ), pl.ds(*cuts[c])]
        return pltpu.make_async_remote_copy(
            src_ref=part,
            dst_ref=part,
            send_sem=gsend.at[d, k, c],
            recv_sem=grecv.at[d, k, c],
            device_id=along_z(lax.rem(z + way + NZ, NZ)),
            device_id_type=MESH,
        )

    def arrived(d, k, c):
        way = 1 if d == 0 else -1
        part = gath.at[lax.rem(z - way * (k + 1) + 2 * NZ, NZ), pl.ds(*cuts[c])]
        pltpu.make_async_remote_copy(
            src_ref=part,
            dst_ref=part,
            send_sem=gsend.at[d, k, c],
            recv_sem=grecv.at[d, k, c],
            device_id=along_z(lax.rem(z + way + NZ, NZ)),
            device_id_type=MESH,
        ).wait_recv()

    def goes(d, k, c):
        return k < NZ // 2 - 1 or c == d

    for c in range(2):
        for d in range(2):
            hop(d, 0, c).start()

    def relay(k):
        for c in range(2):
            for d in range(2):
                if goes(d, k, c):
                    arrived(d, k, c)
                    if k + 1 < NZ // 2 and goes(d, k + 1, c):
                        hop(d, k + 1, c).start()

    for load in loads:
        load.wait()
    own = head_copy
    for q in peers:
        head_copy(q, cot, cots.at[back(q)], c_send, c_recv).wait_recv()
    hgrad[...] = jnp.zeros_like(hgrad)
    for c in range(nx):
        hgrad[...] += jnp.dot(
            jnp.concatenate([cots[2 * c], cots[2 * c + 1]], axis=1),
            w_down[pl.ds(c * 2 * S, 2 * S), :],
            preferred_element_type=F32,
        )
    relay(0)
    for h in range(nhead):
        ctrans[pl.ds(h * S, S), :] = cots[h].astype(F32).T.astype(BF16)
    bpre[3] = compose(bpre[2], block_map(2))
    bpre[5] = compose(bpre[4], block_map(4))
    relay(1)
    bpre[6] = compose(bpre[4], bmaps[1])
    bpre[7] = compose(bpre[6], block_map(6))
    gath[NZ] = none
    table[0] = none
    relay(2)
    relay(3)
    pairs = [compose(gath[2 * i], gath[2 * i + 1]) for i in range(4)]
    table[1] = pairs[0]
    table[2] = pairs[2]
    low = compose(pairs[0], pairs[1])
    table[3] = low
    whole = compose(low, compose(pairs[2], pairs[3]))

    chain = pltpu.make_async_remote_copy(
        src_ref=vout,
        dst_ref=vin,
        send_sem=v_send,
        recv_sem=v_recv,
        device_id=along_y(lax.rem(y + 1, ny)),
        device_id_type=MESH,
    )

    @pl.when(y == 0)
    def _():
        vin[...] = jnp.broadcast_to(init[...], (8, S))

    @pl.when(y > 0)
    def _():
        chain.wait_recv()

    v = vin[0:1, :]

    @pl.when(y < ny - 1)
    def _():
        vout[...] = jnp.broadcast_to(apply_map(v, whole, unit), (8, S))
        chain.start()

    za, zb, zc = lax.div(z, 4), lax.rem(lax.div(z, 2), 2), lax.rem(z, 2)
    v = apply_map(v, table[3 * za], unit)
    v = apply_map(v, table[zb * (1 + za)], unit)
    v = apply_map(v, gath[zc * (z - 1) + (1 - zc) * NZ], unit)
    enter = column(v, unit)

    def block_states(b, _):
        e = jnp.sum(enter * bpre[b, pl.ds(0, S), :], axis=0, keepdims=True) + bpre[b, pl.ds(S, 1), :]
        e = jnp.broadcast_to(column(e, unit), (S, S))
        rows = [
            jnp.sum(e * pre_maps[b * L + step], axis=0, keepdims=True) + shifts[step, pl.ds(b, 1), :]
            for step in range(L)
        ]
        out = jnp.concatenate(rows, axis=0)
        states_out[pl.ds(pl.multiple_of(b * L, L), L), :] = out
        feats[head, pl.ds(pl.multiple_of(b * L, L), L), :] = out.astype(BF16)
        return 0

    lax.fori_loop(0, NB, block_states, 0)

    for q in peers:
        head_copy(q, feats.at[head], feats.at[head], f_send, f_recv).start()
    pre = jnp.zeros(hgrad.shape, F32)
    for dx in [0, 1, nx - 1, 2] if nx >= 4 else range(nx):
        for q in ((dx, 1), (dx, 0)):
            if q != (0, 0):
                head_copy(q, feats.at[head], feats.at[back(q)], f_send, f_recv).wait_recv()
        chip = lax.rem(x + nx - dx, nx)
        both = jnp.concatenate([feats[2 * chip], feats[2 * chip + 1]], axis=1)
        pre = pre + jnp.dot(
            both, w_up[pl.ds(pl.multiple_of(chip * 2 * S, 2 * S), 2 * S), :], preferred_element_type=F32
        )
        ftrans[pl.ds(pl.multiple_of(chip * 2 * S, 2 * S), 2 * S), :] = both.astype(F32).T.astype(BF16)
    gate = jax.nn.sigmoid(pre)
    hidden = (pre * gate).astype(BF16)
    pgrad = (hgrad[...] * gate * (1.0 + pre * (1.0 - gate))).astype(BF16)

    rows = S * nhead // ny
    share = rows // NZ
    for i in range(ny):
        out = jnp.dot(ctrans[pl.ds(i * rows, rows), :], hidden, preferred_element_type=F32).astype(BF16)
        for j in range(NZ):
            dblk[j, pl.ds(i * share, share)] = out[j * share : (j + 1) * share]
    ring_b1 = Ring(NZ, z, along_z, dblk, lb1, b1s, b1r, ny * share // 2)
    ring_b1.begin()
    for i in range(ny):
        ublk[i] = jnp.dot(ftrans[pl.ds(i * rows, rows), :], pgrad, preferred_element_type=F32).astype(BF16)
    ring_a1 = Ring(ny, y, along_y, ublk, la1, a1s, a1r, rows // 2)
    ring_a1.begin()

    for h in range(nhead):
        parts[h, 0] = dot_t(hidden, w_down[pl.ds(h * S, S), :]).astype(BF16)
        parts[h, 1] = dot_t(pgrad, w_up[pl.ds(h * S, S), :]).astype(BF16)
    for q in peers:
        head_copy(q, parts.at[peer(q)], landed.at[head], o_send, o_recv).start()

    ring_b1.advance(0)
    ring_a1.advance(0)
    ring_b1.advance(1)
    ring_a1.advance(1)
    half = rows // 2
    for c in range(2):
        out = ring_a1.total(c).astype(BF16)
        for j in range(NZ // 2):
            u2blk[c * (NZ // 2) + j] = out[j * share : (j + 1) * share]
    ring_a2 = Ring(NZ, z, along_z, u2blk, la2, a2s, a2r, share // 2)
    ring_a2.begin()
    ring_b1.advance(2)
    ring_a2.advance(0)
    ring_b1.advance(3)
    for c in range(2):
        out = ring_b1.total(c).astype(BF16)
        for j in range(ny // 2):
            d2blk[c * (ny // 2) + j] = out[j * share : (j + 1) * share]
    ring_b2 = Ring(ny, y, along_y, d2blk, lb2, b2s, b2r, share // 2)
    ring_b2.begin()
    ring_a2.advance(1)

    for q in peers:
        head_copy(q, parts.at[peer(q)], landed.at[back(q)], o_send, o_recv).wait_recv()
    outs = [parts[head, i].astype(F32) for i in range(2)]
    for q in peers:
        outs = [outs[i] + landed[back(q), i].astype(F32) for i in range(2)]
    mlp_out[...] = outs[0].astype(BF16)
    sgrad_out[...] = outs[1].astype(BF16)

    ring_b2.advance(0)
    ring_a2.advance(2)
    ring_b2.advance(1)
    ring_a2.advance(3)
    for c in range(2):
        gup_out[pl.ds(c * (share // 2), share // 2), :] = ring_a2.total(c)
        gdown_out[pl.ds(c * (share // 2), share // 2), :] = ring_b2.total(c)

    row_copy.wait_send()
    for q in peers:
        head_copy(q, cot, cots.at[head], c_send, c_recv).wait_send()
        head_copy(q, feats.at[head], feats.at[head], f_send, f_recv).wait_send()
        head_copy(q, parts.at[peer(q)], landed.at[head], o_send, o_recv).wait_send()
    for k in range(NZ // 2):
        for d in range(2):
            for c in range(2):
                if goes(d, k, c):
                    hop(d, k, c).wait_send()

    @pl.when(y < ny - 1)
    def _():
        chain.wait_send()

    for ring in (ring_a1, ring_a2, ring_b1, ring_b2):
        ring.finish()


def on_device(ntok, nhead, guess, drive, decay, mixing, init_state, skew_gen, w_up, w_down, cotangent):
    ny = ntok // NZ
    width, ff = w_up.shape
    share = width // ntok
    vm = pl.BlockSpec(memory_space=pltpu.VMEM)
    dma = pltpu.SemaphoreType.DMA
    landing = lambda n, half: pltpu.VMEM((2, n // 2, 2, half, ff), BF16)
    sems = lambda n: dma((2, n // 2, 2))
    scratch = [
        pltpu.VMEM((width, ff), BF16),
        pltpu.VMEM((width, ff), BF16),
        dma((2,)),
        pltpu.VMEM((S + 8, S), F32),
        dma,
        dma,
        pltpu.VMEM((S, S), F32),
        pltpu.VMEM((2 * S, 2 * S), BF16),
        pltpu.VMEM((S, S), F32),
        pltpu.VMEM((S, S), F32),
        pltpu.VMEM((S, S, S), F32),
        pltpu.VMEM((L, NB, S), F32),
        pltpu.VMEM((4, MR, S), F32),
        pltpu.VMEM((NB, MR, S), F32),
        pltpu.VMEM((NZ + 1, MR, S), F32),
        dma((2, NZ // 2, 2)),
        dma((2, NZ // 2, 2)),
        pltpu.VMEM((4, MR, S), F32),
        pltpu.VMEM((8, S), F32),
        pltpu.VMEM((8, S), F32),
        dma,
        dma,
        pltpu.VMEM((nhead, S, S), BF16),
        dma((nhead,)),
        dma((nhead,)),
        pltpu.VMEM((nhead, S, S), BF16),
        dma((nhead,)),
        dma((nhead,)),
        pltpu.VMEM((S, ff), F32),
        pltpu.VMEM((width, S), BF16),
        pltpu.VMEM((width, S), BF16),
        pltpu.VMEM((nhead, 2, S, S), BF16),
        pltpu.VMEM((nhead, 2, S, S), BF16),
        dma((nhead,)),
        dma((nhead,)),
        pltpu.VMEM((ny, NZ * share, ff), BF16),
        pltpu.VMEM((NZ, ny * share, ff), BF16),
        pltpu.VMEM((NZ, share, ff), BF16),
        pltpu.VMEM((ny, share, ff), BF16),
        landing(ny, NZ * share // 2),
        landing(NZ, share // 2),
        landing(NZ, ny * share // 2),
        landing(ny, share // 2),
        sems(ny),
        sems(ny),
        sems(NZ),
        sems(NZ),
        sems(NZ),
        sems(NZ),
        sems(ny),
        sems(ny),
    ]
    return pl.pallas_call(
        functools.partial(kernel, ntok, nhead),
        out_shape=(
            jax.ShapeDtypeStruct((S, S), F32),
            jax.ShapeDtypeStruct((S, S), BF16),
            jax.ShapeDtypeStruct((S, S), BF16),
            jax.ShapeDtypeStruct((share, ff), F32),
            jax.ShapeDtypeStruct((share, ff), F32),
        ),
        in_specs=[vm] * 6 + [pl.BlockSpec(memory_space=pl.ANY)] * 2 + [vm],
        out_specs=[vm] * 5,
        scratch_shapes=scratch,
        compiler_params=pltpu.CompilerParams(
            collective_id=0, has_side_effects=True, vmem_limit_bytes=56 * 1024 * 1024
        ),
    )(
        guess,
        drive,
        decay,
        mixing.reshape(1, S),
        init_state.reshape(1, S),
        skew_gen.reshape(S, S),
        w_up,
        w_down,
        cotangent,
    )


def solution(mesh):
    placed = (
        P("tok", "head"),
        P("tok", "head"),
        P("tok", "head"),
        P("head"),
        P("head"),
        P("head", None, None),
        P(None, "head"),
        P(None, "head"),
        P("tok", "head"),
    )
    return jax.shard_map(
        functools.partial(on_device, mesh.shape["tok"], mesh.shape["head"]),
        mesh=mesh,
        in_specs=placed,
        out_specs=(P("tok", "head"),) * 5,
        check_vma=False,
    )
```

```python
import functools

import jax
import jax.numpy as jnp
from jax import lax
from jax.experimental import pallas as pl
from jax.experimental.pallas import tpu as pltpu
from jax.sharding import PartitionSpec as P

MESH = pl.DeviceIdType.MESH
F32, BF16 = jnp.float32, jnp.bfloat16
S = 128
NZ = 8
NB, L = 8, 16
MR = 144
SENT = 136
CUTS = ((0, 40), (40, 32), (72, 32), (104, 32))
NEWTON = 14
PIECES = 4
ORDER = (4, 3, 6, 1, 5, 2, 7, 0)
TURN = (2, 3, 1, 0)


def split(x):
    hi = x.astype(BF16)
    return hi, (x - hi.astype(F32)).astype(BF16)


def left(x):
    return jnp.concatenate(split(x), axis=1)


def right(x):
    both = jnp.concatenate(split(x), axis=1)
    return jnp.concatenate([both, both], axis=0)


def product(l, r):
    out = jnp.dot(l, r, preferred_element_type=F32)
    return out[:, :S] + out[:, S:]


def mm(a, b):
    return product(left(a), right(b))


def compose(first, then):
    out = mm(first, then[:S])
    return jnp.concatenate([out[:S], out[S:] + then[S:]], axis=0)


def eye():
    rows = lax.broadcasted_iota(jnp.int32, (S, S), 0)
    cols = lax.broadcasted_iota(jnp.int32, (S, S), 1)
    return jnp.where(rows == cols, 1.0, 0.0).astype(F32)


def column(v, unit):
    return jnp.sum(unit * v, axis=1, keepdims=True)


def apply_map(v, m, unit):
    return jnp.sum(column(v, unit) * m[:S], axis=0, keepdims=True) + m[S : S + 1]


def dot_t(a, b):
    return lax.dot_general(a, b, (((1,), (1,)), ((), ())), preferred_element_type=F32)


class Ring:
    def __init__(self, n, me, device, blocks, landing, send, recv):
        self.n, self.me, self.device = n, me, device
        self.blocks, self.landing, self.send, self.recv = blocks, landing, send, recv
        self.rows = blocks.shape[1] // PIECES

    def owner(self, d, hop):
        way = 1 if d == 0 else -1
        return lax.rem(self.me + way * (self.n // 2 - hop) + 2 * self.n, self.n)

    def at(self, c):
        return pl.ds(c * self.rows, self.rows)

    def copy(self, d, hop, c):
        target = lax.rem(self.me + (1 if d == 0 else -1) + self.n, self.n)
        return pltpu.make_async_remote_copy(
            src_ref=self.blocks.at[self.owner(d, hop), self.at(c)],
            dst_ref=self.landing.at[d, hop, c],
            send_sem=self.send.at[d, hop, c],
            recv_sem=self.recv.at[d, hop, c],
            device_id=self.device(target),
            device_id_type=MESH,
        )

    @staticmethod
    def first(d):
        return (0, 1) if d == 0 else (2, 3)

    def begin(self):
        for i in range(2):
            for d in range(2):
                self.copy(d, 0, self.first(d)[i]).start()
        for i in range(2):
            for d in range(2):
                self.copy(d, 1, self.first(1 - d)[i]).start()

    def advance(self, hop, early):
        for i in range(2):
            for d in range(2):
                c = self.first(1 - d if early else d)[i]
                self.copy(d, hop, c).wait_recv()
                to = self.owner(d, hop + 1)
                self.blocks[to, self.at(c)] = (
                    self.blocks[to, self.at(c)].astype(F32) + self.landing[d, hop, c].astype(F32)
                ).astype(BF16)
                self.copy(d, hop + 1, c).start()

    def total(self, c):
        last = self.n // 2 - 1
        out = self.blocks[self.me, self.at(c)].astype(F32)
        for d in range(2):
            self.copy(d, last, c).wait_recv()
            out = out + self.landing[d, last, c].astype(F32)
        return out

    def finish(self):
        for hop in range(self.n // 2):
            for d in range(2):
                for c in self.first(d) if hop == 0 else range(PIECES):
                    self.copy(d, hop, c).wait_send()


def kernel(
    ntok,
    nhead,
    guess,
    drive,
    decay,
    mixing,
    init,
    skew,
    w_up_hbm,
    w_down_hbm,
    cot,
    states_out,
    mlp_out,
    sgrad_out,
    gup_out,
    gdown_out,
    w_up,
    w_down,
    w_sem,
    shifted,
    row_send,
    row_recv,
    wrot,
    slopes,
    offs,
    pre_maps,
    shifts,
    bmaps,
    bpre,
    gath,
    gsend,
    grecv,
    table,
    vin,
    vout,
    tin,
    tout,
    v_send,
    v_recv,
    feats,
    f_send,
    f_recv,
    cots,
    c_send,
    c_recv,
    hgrad,
    hidden,
    pgrad,
    ftrans,
    ctrans,
    parts,
    landed,
    o_send,
    o_recv,
    ublk,
    dblk,
    u2blk,
    d2blk,
    la1,
    la2,
    lb1,
    lb2,
    a1s,
    a1r,
    a2s,
    a2r,
    b1s,
    b1r,
    b2s,
    b2r,
):
    ny, nx = ntok // NZ, nhead // 2
    tok, head = lax.axis_index("tok"), lax.axis_index("head")
    y, z = lax.div(tok, NZ), lax.rem(tok, NZ)
    x, core = lax.div(head, 2), lax.rem(head, 2)

    def along_z(target):
        return {"tok": y * NZ + target, "head": head}

    def along_y(target):
        return {"tok": target * NZ + z, "head": head}

    def at_tok(target):
        return {"tok": target, "head": head}

    def at_head(target):
        return {"tok": tok, "head": target}

    peers = [(dx, flip) for dx in ([0, 1, nx - 1, 2] if nx >= 4 else range(nx)) for flip in (1, 0)]
    peers = [q for q in peers if q != (0, 0)]

    def peer(q):
        return lax.rem(x + q[0], nx) * 2 + lax.rem(core + q[1], 2)

    after, before_me = lax.rem(tok + 1, ntok), lax.rem(tok + ntok - 1, ntok)

    barrier = pltpu.get_barrier_semaphore()
    greet = [along_z(lax.rem(z + 1, NZ)), along_z(lax.rem(z + NZ - 1, NZ))]
    greet += [along_y(lax.rem(y + i, ny)) for i in range(1, ny)]
    greet += [at_tok(after), at_tok(before_me)]
    greet += [at_head(peer(q)) for q in peers]
    for who in greet:
        pl.semaphore_signal(barrier, inc=1, device_id=who, device_id_type=MESH)
    loads = [
        pltpu.make_async_copy(w_up_hbm, w_up, w_sem.at[0]),
        pltpu.make_async_copy(w_down_hbm, w_down, w_sem.at[1]),
    ]
    for load in loads:
        load.start()

    unit = eye()
    k = skew[...]
    a = unit + k
    kk = mm(k, k)
    bound = jnp.sqrt(jnp.sum(jnp.sum(kk * kk, axis=1, keepdims=True), axis=0, keepdims=True) * 0.5)
    top = 1.0 + 1.01 * bound
    scale = 2.0 / (1.0 + top)
    gap = (top - 1.0) / (top + 1.0)

    def newton(v, t, gap):
        square = gap * gap
        wide = 2.0 / (2.0 - square)
        out = product(left(jnp.concatenate([t, v], axis=0)), right(wide * (2.0 * unit - t)))
        return out[S:], out[:S], square / (2.0 - square)

    v, t = (unit - k) * scale, (unit - kk) * scale
    for _ in range(NEWTON // 2):
        v, t, gap = newton(v, t, gap)

    pl.semaphore_wait(barrier, len(greet))
    row_copy = pltpu.make_async_remote_copy(
        src_ref=guess.at[pl.ds(S - 8, 8)],
        dst_ref=shifted.at[pl.ds(0, 8)],
        send_sem=row_send,
        recv_sem=row_recv,
        device_id=at_tok(after),
        device_id_type=MESH,
    )
    row_copy.start()

    def head_copy(q, src, dst, send, recv):
        return pltpu.make_async_remote_copy(
            src_ref=src,
            dst_ref=dst,
            send_sem=send.at[q[0] * 2 + q[1]],
            recv_sem=recv.at[q[0] * 2 + q[1]],
            device_id=at_head(peer(q)),
            device_id_type=MESH,
        )

    def back(q):
        return lax.rem(x + nx - q[0], nx) * 2 + lax.rem(core + q[1], 2)

    for q in peers:
        head_copy(q, cot, cots.at[head], c_send, c_recv).start()
    cots[head] = cot[...]

    for _ in range(NEWTON - NEWTON // 2):
        v, t, gap = newton(v, t, gap)
    t = jnp.dot(a, v, precision=lax.Precision.HIGHEST, preferred_element_type=F32)
    v = v + mm(v, unit - t)
    rot_t = 2.0 * v - unit
    wrot[...] = right(rot_t)

    shifted[pl.ds(8, S), :] = guess[...]
    row_copy.wait_recv()
    before = shifted[pl.ds(7, S), :]
    first = (lax.broadcasted_iota(jnp.int32, (S, S), 0) == 0) & (tok == 0)
    before = jnp.where(first, init[...], before)
    m = mixing[...]
    bent = jnp.tanh(before)
    curve = 1.0 - bent * bent
    slopes[...] = (1.0 - m) * decay[...] + m * curve
    offs[...] = product(left(m * (bent - curve * before)), wrot[...]) + drive[...]

    def advance(step, blocks, shift):
        rows = [left(blocks[b] * slopes[pl.ds(b * L + step, 1), :]) for b in range(NB)]
        shift = shift * slopes[pl.ds(step, NB, stride=L), :]
        rows.append(left(jnp.concatenate([shift, jnp.zeros((16 - NB, S), F32)], axis=0)))
        out = product(jnp.concatenate(rows, axis=0), wrot[...])
        for b in range(NB):
            pre_maps[b * L + step] = out[b * S : (b + 1) * S]
        shifts[step] = out[NB * S : NB * S + NB] + offs[pl.ds(step, NB, stride=L), :]

    advance(0, [unit] * NB, jnp.zeros((NB, S), F32))

    for step in range(1, L):
        advance(step, [pre_maps[b * L + step - 1] for b in range(NB)], shifts[step - 1])

    pad = jnp.zeros((MR - S - 1, S), F32)

    def block_map(b):
        return jnp.concatenate([pre_maps[b * L + L - 1], shifts[L - 1, b : b + 1], pad], axis=0)

    none = jnp.concatenate([unit, jnp.zeros((MR - S, S), F32)], axis=0)
    bpre[0] = none
    bpre[1] = block_map(0)
    bpre[2] = compose(block_map(0), block_map(1))
    bmaps[0] = compose(block_map(2), block_map(3))
    bmaps[1] = compose(block_map(4), block_map(5))
    bmaps[2] = compose(block_map(6), block_map(7))
    bpre[4] = compose(bpre[2], bmaps[0])
    bmaps[3] = compose(bmaps[1], bmaps[2])
    gath[z] = compose(bpre[4], bmaps[3])

    def hop(d, k, c, arriving=0):
        way = 1 if d == 0 else -1
        part = gath.at[lax.rem(z - way * (k + arriving) + 2 * NZ, NZ), pl.ds(*CUTS[c])]
        return pltpu.make_async_remote_copy(
            src_ref=part,
            dst_ref=part,
            send_sem=gsend.at[d, k, c],
            recv_sem=grecv.at[d, k, c],
            device_id=along_z(lax.rem(z + way + NZ, NZ)),
            device_id_type=MESH,
        )

    def goes(d, k, c):
        return k < NZ // 2 - 1 or c // 2 == d

    turns = [(d, c if d == 0 else (c + 2) % 4) for c in range(4) for d in range(2)]
    for d, c in turns:
        hop(d, 0, c).start()

    def relay(k):
        for d, c in turns:
            if goes(d, k, c):
                hop(d, k, c, 1).wait_recv()
                if k + 1 < NZ // 2 and goes(d, k + 1, c):
                    hop(d, k + 1, c).start()

    for load in loads:
        load.wait()
    for q in peers:
        head_copy(q, cot, cots.at[back(q)], c_send, c_recv).wait_recv()
    hgrad[...] = jnp.zeros_like(hgrad)
    for c in range(nx):
        hgrad[...] += jnp.dot(
            jnp.concatenate([cots[2 * c], cots[2 * c + 1]], axis=1),
            w_down[pl.ds(c * 2 * S, 2 * S), :],
            preferred_element_type=F32,
        )
    relay(0)
    for h in range(nhead):
        ctrans[pl.ds(h * S, S), :] = cots[h].astype(F32).T.astype(BF16)
    bpre[3] = compose(bpre[2], block_map(2))
    bpre[5] = compose(bpre[4], block_map(4))
    relay(1)
    bpre[6] = compose(bpre[4], bmaps[1])
    bpre[7] = compose(bpre[6], block_map(6))
    gath[NZ] = none
    table[0] = none
    relay(2)
    relay(3)
    pairs = [compose(gath[2 * i], gath[2 * i + 1]) for i in range(4)]
    table[1] = pairs[0]
    table[2] = pairs[2]
    low = compose(pairs[0], pairs[1])
    table[3] = low
    whole = compose(low, compose(pairs[2], pairs[3]))

    def chain(i, target):
        return pltpu.make_async_remote_copy(
            src_ref=vout,
            dst_ref=vin,
            send_sem=v_send.at[i],
            recv_sem=v_recv.at[0],
            device_id=along_y(target),
            device_id_type=MESH,
        )

    carry = pltpu.make_async_remote_copy(
        src_ref=tout.at[pl.ds(0, SENT)],
        dst_ref=tin.at[pl.ds(0, SENT)],
        send_sem=v_send.at[2],
        recv_sem=v_recv.at[1],
        device_id=along_y(3),
        device_id_type=MESH,
    )

    @pl.when(y == 2)
    def _():
        tout[...] = whole
        carry.start()

    @pl.when(y == 0)
    def _():
        vin[...] = jnp.broadcast_to(init[...], (8, S))
        vout[...] = jnp.broadcast_to(apply_map(init[...], whole, unit), (8, S))
        chain(0, 1).start()

    @pl.when(y > 0)
    def _():
        chain(0, 1).wait_recv()

    @pl.when(y == 1)
    def _():
        vout[...] = jnp.broadcast_to(apply_map(vin[0:1, :], whole, unit), (8, S))
        chain(0, 3).start()
        chain(1, 2).start()

    @pl.when(y == 3)
    def _():
        carry.wait_recv()
        vin[...] = jnp.broadcast_to(apply_map(vin[0:1, :], tin, unit), (8, S))

    v = vin[0:1, :]
    za, zb, zc = lax.div(z, 4), lax.rem(lax.div(z, 2), 2), lax.rem(z, 2)
    v = apply_map(v, table[3 * za], unit)
    v = apply_map(v, table[zb * (1 + za)], unit)
    v = apply_map(v, gath[zc * (z - 1) + (1 - zc) * NZ], unit)
    enter = column(v, unit)

    half = S // 2

    def feat_copy(q, part, who):
        return pltpu.make_async_remote_copy(
            src_ref=feats.at[head, pl.ds(part * half, half)],
            dst_ref=feats.at[who, pl.ds(part * half, half)],
            send_sem=f_send.at[part, q[0] * 2 + q[1]],
            recv_sem=f_recv.at[part, q[0] * 2 + q[1]],
            device_id=at_head(peer(q)),
            device_id_type=MESH,
        )

    for b in range(NB):
        e = jnp.sum(enter * bpre[b, 0:S, :], axis=0, keepdims=True) + bpre[b, S : S + 1, :]
        e = jnp.broadcast_to(column(e, unit), (S, S))
        rows = [
            jnp.sum(e * pre_maps[b * L + step], axis=0, keepdims=True) + shifts[step, b : b + 1, :]
            for step in range(L)
        ]
        out = jnp.concatenate(rows, axis=0)
        states_out[b * L : (b + 1) * L, :] = out
        feats[head, b * L : (b + 1) * L, :] = out.astype(BF16)
        if b % (NB // 2) == NB // 2 - 1:
            for q in peers:
                feat_copy(q, b // (NB // 2), head).start()

    def of_chip(dx, rows):
        chip = lax.rem(x + nx - dx, nx)
        both = jnp.concatenate([feats[2 * chip, rows], feats[2 * chip + 1, rows]], axis=1)
        return both, pl.ds(pl.multiple_of(chip * 2 * S, 2 * S), 2 * S)

    ring_dx = [0, 1, nx - 1, 2]
    for part in range(2):
        rows = slice(part * half, (part + 1) * half)
        pre = jnp.zeros((half, w_up.shape[1]), F32)
        for dx in ring_dx:
            for q in ((dx, 1), (dx, 0)):
                if q != (0, 0):
                    feat_copy(q, part, back(q)).wait_recv()
            both, cols = of_chip(dx, rows)
            pre = pre + jnp.dot(both, w_up[cols, :], preferred_element_type=F32)
        gate = jax.nn.sigmoid(pre)
        hidden[rows, :] = (pre * gate).astype(BF16)
        pgrad[rows, :] = (hgrad[rows, :] * gate * (1.0 + pre * (1.0 - gate))).astype(BF16)

    rows = S * nhead // ny
    share = rows // NZ
    for i in range(ny):
        out = jnp.dot(ctrans[pl.ds(i * rows, rows), :], hidden[...], preferred_element_type=F32).astype(BF16)
        place = lax.rem(i - y + ny, ny)
        piece = sum(jnp.where(place == t, n, 0) for n, t in enumerate(TURN))
        for j in range(NZ):
            dblk[j, pl.ds(pl.multiple_of(piece * share, share), share)] = out[j * share : (j + 1) * share]
    ring_b1 = Ring(NZ, z, along_z, dblk, lb1, b1s, b1r)
    ring_b1.begin()
    for dx in ring_dx:
        both, cols = of_chip(dx, slice(0, S))
        ftrans[cols, :] = both.astype(F32).T.astype(BF16)
    for i in range(ny):
        out = jnp.dot(ftrans[pl.ds(i * rows, rows), :], pgrad[...], preferred_element_type=F32).astype(BF16)
        for j in range(NZ):
            place = lax.rem(j - z + NZ, NZ)
            piece = sum(jnp.where(place == t, n, 0) for n, t in enumerate(ORDER))
            ublk[i, pl.ds(pl.multiple_of(piece * share, share), share)] = out[j * share : (j + 1) * share]
    ring_a1 = Ring(ny, y, along_y, ublk, la1, a1s, a1r)
    ring_a1.begin()

    for h in range(nhead):
        parts[h, 0] = dot_t(hidden[...], w_down[pl.ds(h * S, S), :]).astype(BF16)
        parts[h, 1] = dot_t(pgrad[...], w_up[pl.ds(h * S, S), :]).astype(BF16)
    for q in peers:
        head_copy(q, parts.at[peer(q)], landed.at[head], o_send, o_recv).start()

    def up_copy(r):
        return pltpu.make_async_remote_copy(
            src_ref=u2blk.at[r],
            dst_ref=la2.at[r],
            send_sem=a2s.at[r],
            recv_sem=a2r.at[r],
            device_id=along_z(lax.rem(z + r, NZ)),
            device_id_type=MESH,
        )

    def up_part(c):
        out = ring_a1.total(c)
        for i in range(2):
            r = ORDER[2 * c + i]
            mine = out[i * share : (i + 1) * share]
            if r == 0:
                gup_out[...] = mine
            else:
                u2blk[r] = mine.astype(BF16)
                up_copy(r).start()

    def down_copy(r):
        return pltpu.make_async_remote_copy(
            src_ref=d2blk.at[r],
            dst_ref=lb2.at[r],
            send_sem=b2s.at[r],
            recv_sem=b2r.at[r],
            device_id=along_y(lax.rem(y + r, ny)),
            device_id_type=MESH,
        )

    def down_part(c):
        out = ring_b1.total(c)
        r = TURN[c]
        if r == 0:
            gdown_out[...] = out
        else:
            d2blk[r] = out.astype(BF16)
            down_copy(r).start()

    ring_b1.advance(0, False)
    ring_a1.advance(0, False)
    ring_b1.advance(1, True)
    ring_b1.advance(1, False)
    ring_b1.advance(2, True)
    ring_b1.advance(2, False)
    for q in peers:
        head_copy(q, parts.at[peer(q)], landed.at[back(q)], o_send, o_recv).wait_recv()
    outs = [parts[head, i].astype(F32) for i in range(2)]
    for q in peers:
        outs = [outs[i] + landed[back(q), i].astype(F32) for i in range(2)]
    mlp_out[...] = outs[0].astype(BF16)
    sgrad_out[...] = outs[1].astype(BF16)
    up_part(0)
    up_part(2)
    up_part(1)
    up_part(3)
    for c in (0, 2, 1, 3):
        down_part(c)
    for r in (1, 7, 2, 6, 3, 5, 4):
        up_copy(r).wait_recv()
        gup_out[...] += la2[r].astype(F32)
    for r in (1, 3, 2):
        down_copy(r).wait_recv()
        gdown_out[...] += lb2[r].astype(F32)

    row_copy.wait_send()
    for q in peers:
        head_copy(q, cot, cots.at[head], c_send, c_recv).wait_send()
        for part in range(2):
            feat_copy(q, part, head).wait_send()
        head_copy(q, parts.at[peer(q)], landed.at[head], o_send, o_recv).wait_send()
    for k in range(NZ // 2):
        for d in range(2):
            for c in range(len(CUTS)):
                if goes(d, k, c):
                    hop(d, k, c).wait_send()

    @pl.when(y < 2)
    def _():
        chain(0, 1).wait_send()

    @pl.when(y == 1)
    def _():
        chain(1, 2).wait_send()

    @pl.when(y == 2)
    def _():
        carry.wait_send()

    for ring in (ring_a1, ring_b1):
        ring.finish()
    for r in range(1, NZ):
        up_copy(r).wait_send()
    for r in range(1, ny):
        down_copy(r).wait_send()


def settle(*refs):
    for src, dst in zip(refs[:5], refs[5:]):
        dst[...] = src[...]


def on_device(ntok, nhead, guess, drive, decay, mixing, init_state, skew_gen, w_up, w_down, cotangent):
    ny = ntok // NZ
    width, ff = w_up.shape
    share = width // ntok
    vm = pl.BlockSpec(memory_space=pltpu.VMEM)
    dma = pltpu.SemaphoreType.DMA
    landing = lambda n, rows: pltpu.VMEM((2, n // 2, PIECES, rows // PIECES, ff), BF16)
    sems = lambda n: dma((2, n // 2, PIECES))
    scratch = [
        pltpu.VMEM((width, ff), BF16),
        pltpu.VMEM((width, ff), BF16),
        dma((2,)),
        pltpu.VMEM((S + 8, S), F32),
        dma,
        dma,
        pltpu.VMEM((2 * S, 2 * S), BF16),
        pltpu.VMEM((S, S), F32),
        pltpu.VMEM((S, S), F32),
        pltpu.VMEM((S, S, S), F32),
        pltpu.VMEM((L, NB, S), F32),
        pltpu.VMEM((4, MR, S), F32),
        pltpu.VMEM((NB, MR, S), F32),
        pltpu.VMEM((NZ + 1, MR, S), F32),
        dma((2, NZ // 2, len(CUTS))),
        dma((2, NZ // 2, len(CUTS))),
        pltpu.VMEM((4, MR, S), F32),
        pltpu.VMEM((8, S), F32),
        pltpu.VMEM((8, S), F32),
        pltpu.VMEM((MR, S), F32),
        pltpu.VMEM((MR, S), F32),
        dma((3,)),
        dma((2,)),
        pltpu.VMEM((nhead, S, S), BF16),
        dma((2, nhead)),
        dma((2, nhead)),
        pltpu.VMEM((nhead, S, S), BF16),
        dma((nhead,)),
        dma((nhead,)),
        pltpu.VMEM((S, ff), F32),
        pltpu.VMEM((S, ff), BF16),
        pltpu.VMEM((S, ff), BF16),
        pltpu.VMEM((width, S), BF16),
        pltpu.VMEM((width, S), BF16),
        pltpu.VMEM((nhead, 2, S, S), BF16),
        pltpu.VMEM((nhead, 2, S, S), BF16),
        dma((nhead,)),
        dma((nhead,)),
        pltpu.VMEM((ny, NZ * share, ff), BF16),
        pltpu.VMEM((NZ, ny * share, ff), BF16),
        pltpu.VMEM((NZ, share, ff), BF16),
        pltpu.VMEM((ny, share, ff), BF16),
        landing(ny, NZ * share),
        pltpu.VMEM((NZ, share, ff), BF16),
        landing(NZ, ny * share),
        pltpu.VMEM((ny, share, ff), BF16),
        sems(ny),
        sems(ny),
        dma((NZ,)),
        dma((NZ,)),
        sems(NZ),
        sems(NZ),
        dma((ny,)),
        dma((ny,)),
    ]
    results = [((S, S), F32), ((S, S), BF16), ((S, S), BF16), ((share, ff), F32), ((share, ff), F32)]
    done = pl.pallas_call(
        functools.partial(kernel, ntok, nhead),
        out_shape=tuple(pltpu.VMEM(*r) for r in results),
        in_specs=[vm] * 6 + [pl.BlockSpec(memory_space=pl.ANY)] * 2 + [vm],
        out_specs=[vm] * 5,
        scratch_shapes=scratch,
        compiler_params=pltpu.CompilerParams(
            collective_id=0, has_side_effects=True, vmem_limit_bytes=56 * 1024 * 1024
        ),
    )(
        guess,
        drive,
        decay,
        mixing.reshape(1, S),
        init_state.reshape(1, S),
        skew_gen.reshape(S, S),
        w_up,
        w_down,
        cotangent,
    )
    return pl.pallas_call(
        settle,
        out_shape=tuple(jax.ShapeDtypeStruct(*r) for r in results),
        in_specs=[vm] * 5,
        out_specs=[vm] * 5,
    )(*[pltpu.with_memory_space_constraint(d, pltpu.VMEM) for d in done])


def solution(mesh):
    placed = (
        P("tok", "head"),
        P("tok", "head"),
        P("tok", "head"),
        P("head"),
        P("head"),
        P("head", None, None),
        P(None, "head"),
        P(None, "head"),
        P("tok", "head"),
    )
    return jax.shard_map(
        functools.partial(on_device, mesh.shape["tok"], mesh.shape["head"]),
        mesh=mesh,
        in_specs=placed,
        out_specs=(P("tok", "head"),) * 5,
        check_vma=False,
    )
```

```python
import functools

import jax
import jax.numpy as jnp
from jax import lax
from jax.experimental import pallas as pl
from jax.experimental.pallas import tpu as pltpu
from jax.sharding import PartitionSpec as P

MESH = pl.DeviceIdType.MESH
F32, BF16 = jnp.float32, jnp.bfloat16
S = 128
NZ = 8
NB, L = 8, 16
MR = 144
SENT = 136
CUTS = ((0, 72), (72, 64))
LEGS = ((2, 0), (-2, 0), (1, 0), (-1, 0), (1, -2), (-1, 2), (2, -2), (-2, 2))
NEWTON = 14
PIECES = 4
ORDER = (4, 3, 6, 1, 5, 2, 7, 0)
TURN = (2, 3, 1, 0)


def split(x):
    hi = x.astype(BF16)
    return hi, (x - hi.astype(F32)).astype(BF16)


def left(x):
    return jnp.concatenate(split(x), axis=1)


def right(x):
    both = jnp.concatenate(split(x), axis=1)
    return jnp.concatenate([both, both], axis=0)


def product(l, r):
    out = jnp.dot(l, r, preferred_element_type=F32)
    return out[:, :S] + out[:, S:]


def mm(a, b):
    return product(left(a), right(b))


def compose(first, then):
    out = mm(first, then[:S])
    return jnp.concatenate([out[:S], out[S:] + then[S:]], axis=0)


def eye():
    rows = lax.broadcasted_iota(jnp.int32, (S, S), 0)
    cols = lax.broadcasted_iota(jnp.int32, (S, S), 1)
    return jnp.where(rows == cols, 1.0, 0.0).astype(F32)


def column(v, unit):
    return jnp.sum(unit * v, axis=1, keepdims=True)


def apply_map(v, m, unit):
    return jnp.sum(column(v, unit) * m[:S], axis=0, keepdims=True) + m[S : S + 1]


def dot_t(a, b):
    return lax.dot_general(a, b, (((1,), (1,)), ((), ())), preferred_element_type=F32)


class Ring:
    def __init__(self, n, me, device, blocks, landing, send, recv):
        self.n, self.me, self.device = n, me, device
        self.blocks, self.landing, self.send, self.recv = blocks, landing, send, recv
        self.rows = blocks.shape[1] // PIECES

    def owner(self, d, hop):
        way = 1 if d == 0 else -1
        return lax.rem(self.me + way * (self.n // 2 - hop) + 2 * self.n, self.n)

    def at(self, c):
        return pl.ds(c * self.rows, self.rows)

    def copy(self, d, hop, c):
        target = lax.rem(self.me + (1 if d == 0 else -1) + self.n, self.n)
        return pltpu.make_async_remote_copy(
            src_ref=self.blocks.at[self.owner(d, hop), self.at(c)],
            dst_ref=self.landing.at[d, hop, c],
            send_sem=self.send.at[d, hop, c],
            recv_sem=self.recv.at[d, hop, c],
            device_id=self.device(target),
            device_id_type=MESH,
        )

    @staticmethod
    def first(d):
        return (0, 1) if d == 0 else (2, 3)

    def begin(self):
        for i in range(2):
            for d in range(2):
                self.copy(d, 0, self.first(d)[i]).start()
        for i in range(2):
            for d in range(2):
                self.copy(d, 1, self.first(1 - d)[i]).start()

    def advance(self, hop, early):
        for i in range(2):
            for d in range(2):
                c = self.first(1 - d if early else d)[i]
                self.copy(d, hop, c).wait_recv()
                to = self.owner(d, hop + 1)
                self.blocks[to, self.at(c)] = (
                    self.blocks[to, self.at(c)].astype(F32) + self.landing[d, hop, c].astype(F32)
                ).astype(BF16)
                self.copy(d, hop + 1, c).start()

    def total(self, c):
        last = self.n // 2 - 1
        out = self.blocks[self.me, self.at(c)].astype(F32)
        for d in range(2):
            self.copy(d, last, c).wait_recv()
            out = out + self.landing[d, last, c].astype(F32)
        return out

    def finish(self):
        for hop in range(self.n // 2):
            for d in range(2):
                for c in self.first(d) if hop == 0 else range(PIECES):
                    self.copy(d, hop, c).wait_send()


def kernel(
    ntok,
    nhead,
    guess,
    drive,
    decay,
    mixing,
    init,
    skew,
    w_up_hbm,
    w_down_hbm,
    cot,
    states_out,
    mlp_out,
    sgrad_out,
    gup_out,
    gdown_out,
    w_up,
    w_down,
    w_sem,
    shifted,
    row_send,
    row_recv,
    wrot,
    slopes,
    offs,
    pre_maps,
    shifts,
    bmaps,
    bpre,
    gath,
    gsend,
    grecv,
    table,
    vin,
    vout,
    tin,
    tout,
    v_send,
    v_recv,
    feats,
    f_send,
    f_recv,
    cots,
    c_send,
    c_recv,
    hgrad,
    hidden,
    pgrad,
    ftrans,
    ctrans,
    parts,
    landed,
    o_send,
    o_recv,
    ublk,
    dblk,
    u2blk,
    d2blk,
    la1,
    la2,
    lb1,
    lb2,
    a1s,
    a1r,
    a2s,
    a2r,
    b1s,
    b1r,
    b2s,
    b2r,
):
    ny, nx = ntok // NZ, nhead // 2
    tok, head = lax.axis_index("tok"), lax.axis_index("head")
    y, z = lax.div(tok, NZ), lax.rem(tok, NZ)
    x, core = lax.div(head, 2), lax.rem(head, 2)

    def along_z(target):
        return {"tok": y * NZ + target, "head": head}

    def along_y(target):
        return {"tok": target * NZ + z, "head": head}

    def at_tok(target):
        return {"tok": target, "head": head}

    def at_head(target):
        return {"tok": tok, "head": target}

    peers = [(dx, flip) for dx in ([0, 1, nx - 1, 2] if nx >= 4 else range(nx)) for flip in (1, 0)]
    peers = [q for q in peers if q != (0, 0)]

    def peer(q):
        return lax.rem(x + q[0], nx) * 2 + lax.rem(core + q[1], 2)

    after, before_me = lax.rem(tok + 1, ntok), lax.rem(tok + ntok - 1, ntok)

    barrier = pltpu.get_barrier_semaphore()
    greet = [along_z(lax.rem(z + i, NZ)) for i in (1, 2, NZ - 1, NZ - 2)]
    greet += [along_y(lax.rem(y + i, ny)) for i in range(1, ny)]
    greet += [at_tok(after), at_tok(before_me)]
    greet += [at_head(peer(q)) for q in peers]
    for who in greet:
        pl.semaphore_signal(barrier, inc=1, device_id=who, device_id_type=MESH)
    loads = [
        pltpu.make_async_copy(w_up_hbm, w_up, w_sem.at[0]),
        pltpu.make_async_copy(w_down_hbm, w_down, w_sem.at[1]),
    ]
    for load in loads:
        load.start()

    unit = eye()
    k = skew[...]
    a = unit + k
    kk = mm(k, k)
    bound = jnp.sqrt(jnp.sum(jnp.sum(kk * kk, axis=1, keepdims=True), axis=0, keepdims=True) * 0.5)
    top = 1.0 + 1.01 * bound
    scale = 2.0 / (1.0 + top)
    gap = (top - 1.0) / (top + 1.0)

    def newton(v, t, gap):
        square = gap * gap
        wide = 2.0 / (2.0 - square)
        out = product(left(jnp.concatenate([t, v], axis=0)), right(wide * (2.0 * unit - t)))
        return out[S:], out[:S], square / (2.0 - square)

    v, t = (unit - k) * scale, (unit - kk) * scale
    for _ in range(NEWTON // 2):
        v, t, gap = newton(v, t, gap)

    pl.semaphore_wait(barrier, len(greet))
    row_copy = pltpu.make_async_remote_copy(
        src_ref=guess.at[pl.ds(S - 8, 8)],
        dst_ref=shifted.at[pl.ds(0, 8)],
        send_sem=row_send,
        recv_sem=row_recv,
        device_id=at_tok(after),
        device_id_type=MESH,
    )
    row_copy.start()

    def head_copy(q, src, dst, send, recv):
        return pltpu.make_async_remote_copy(
            src_ref=src,
            dst_ref=dst,
            send_sem=send.at[q[0] * 2 + q[1]],
            recv_sem=recv.at[q[0] * 2 + q[1]],
            device_id=at_head(peer(q)),
            device_id_type=MESH,
        )

    def back(q):
        return lax.rem(x + nx - q[0], nx) * 2 + lax.rem(core + q[1], 2)

    for q in peers:
        head_copy(q, cot, cots.at[head], c_send, c_recv).start()
    cots[head] = cot[...]

    for _ in range(NEWTON - NEWTON // 2):
        v, t, gap = newton(v, t, gap)
    t = jnp.dot(a, v, precision=lax.Precision.HIGHEST, preferred_element_type=F32)
    v = v + mm(v, unit - t)
    rot_t = 2.0 * v - unit
    wrot[...] = right(rot_t)

    shifted[pl.ds(8, S), :] = guess[...]
    row_copy.wait_recv()
    before = shifted[pl.ds(7, S), :]
    first = (lax.broadcasted_iota(jnp.int32, (S, S), 0) == 0) & (tok == 0)
    before = jnp.where(first, init[...], before)
    m = mixing[...]
    bent = jnp.tanh(before)
    curve = 1.0 - bent * bent
    slopes[...] = (1.0 - m) * decay[...] + m * curve
    offs[...] = product(left(m * (bent - curve * before)), wrot[...]) + drive[...]

    def advance(step, blocks, shift):
        rows = [left(blocks[b] * slopes[pl.ds(b * L + step, 1), :]) for b in range(NB)]
        shift = shift * slopes[pl.ds(step, NB, stride=L), :]
        rows.append(left(jnp.concatenate([shift, jnp.zeros((16 - NB, S), F32)], axis=0)))
        out = product(jnp.concatenate(rows, axis=0), wrot[...])
        for b in range(NB):
            pre_maps[b * L + step] = out[b * S : (b + 1) * S]
        shifts[step] = out[NB * S : NB * S + NB] + offs[pl.ds(step, NB, stride=L), :]

    advance(0, [unit] * NB, jnp.zeros((NB, S), F32))

    for step in range(1, L):
        advance(step, [pre_maps[b * L + step - 1] for b in range(NB)], shifts[step - 1])

    pad = jnp.zeros((MR - S - 1, S), F32)

    def block_map(b):
        return jnp.concatenate([pre_maps[b * L + L - 1], shifts[L - 1, b : b + 1], pad], axis=0)

    none = jnp.concatenate([unit, jnp.zeros((MR - S, S), F32)], axis=0)
    bpre[0] = none
    bpre[1] = block_map(0)
    bpre[2] = compose(block_map(0), block_map(1))
    bmaps[0] = compose(block_map(2), block_map(3))
    bmaps[1] = compose(block_map(4), block_map(5))
    bmaps[2] = compose(block_map(6), block_map(7))
    bpre[4] = compose(bpre[2], bmaps[0])
    bmaps[3] = compose(bmaps[1], bmaps[2])
    gath[z] = compose(bpre[4], bmaps[3])

    def leg(n, c, arriving=False):
        way, owner = LEGS[n]
        owner = owner - way if arriving else owner
        part = gath.at[lax.rem(z + owner + 2 * NZ, NZ), pl.ds(*CUTS[c])]
        return pltpu.make_async_remote_copy(
            src_ref=part,
            dst_ref=part,
            send_sem=gsend.at[n, c],
            recv_sem=grecv.at[n, c],
            device_id=along_z(lax.rem(z + way + NZ, NZ)),
            device_id_type=MESH,
        )

    def legs(n):
        return (n % 2,) if n >= 6 else (0, 1)

    for n in range(4):
        for c in legs(n):
            leg(n, c).start()

    for load in loads:
        load.wait()
    for q in peers:
        head_copy(q, cot, cots.at[back(q)], c_send, c_recv).wait_recv()
    hgrad[...] = jnp.zeros_like(hgrad)
    for c in range(nx):
        hgrad[...] += jnp.dot(
            jnp.concatenate([cots[2 * c], cots[2 * c + 1]], axis=1),
            w_down[pl.ds(c * 2 * S, 2 * S), :],
            preferred_element_type=F32,
        )
    for c in range(2):
        for n in range(2):
            leg(n, c, True).wait_recv()
            if c in legs(6 + n):
                leg(6 + n, c).start()
            leg(4 + n, c).start()
    for h in range(nhead):
        ctrans[pl.ds(h * S, S), :] = cots[h].astype(F32).T.astype(BF16)
    bpre[3] = compose(bpre[2], block_map(2))
    bpre[5] = compose(bpre[4], block_map(4))
    bpre[6] = compose(bpre[4], bmaps[1])
    bpre[7] = compose(bpre[6], block_map(6))
    gath[NZ] = none
    table[0] = none
    for n in range(2, 8):
        for c in legs(n):
            leg(n, c, True).wait_recv()
    pairs = [compose(gath[2 * i], gath[2 * i + 1]) for i in range(4)]
    table[1] = pairs[0]
    table[2] = pairs[2]
    low = compose(pairs[0], pairs[1])
    table[3] = low
    whole = compose(low, compose(pairs[2], pairs[3]))

    def tell_state(row):
        return pltpu.make_async_remote_copy(
            src_ref=vout,
            dst_ref=vin,
            send_sem=v_send.at[row],
            recv_sem=v_recv.at[0],
            device_id=along_y(row),
            device_id_type=MESH,
        )

    def tell_map(row, owner):
        return pltpu.make_async_remote_copy(
            src_ref=tout.at[pl.ds(0, SENT)],
            dst_ref=tin.at[owner - 1, pl.ds(0, SENT)],
            send_sem=v_send.at[row],
            recv_sem=v_recv.at[owner],
            device_id=along_y(row),
            device_id_type=MESH,
        )

    @pl.when(y == 0)
    def _():
        vout[...] = jnp.broadcast_to(apply_map(init[...], whole, unit), (8, S))
        for row in range(ny - 1, 0, -1):
            tell_state(row).start()
        vin[...] = jnp.broadcast_to(init[...], (8, S))

    for owner in range(1, ny - 1):

        @pl.when(y == owner)
        def _():
            tout[...] = whole
            for row in range(ny - 1, owner, -1):
                tell_map(row, owner).start()

    @pl.when(y > 0)
    def _():
        tell_state(1).wait_recv()

    for owner in range(1, ny - 1):

        @pl.when(y > owner)
        def _():
            tell_map(ny - 1, owner).wait_recv()
            vin[...] = jnp.broadcast_to(apply_map(vin[0:1, :], tin[owner - 1], unit), (8, S))

    v = vin[0:1, :]
    za, zb, zc = lax.div(z, 4), lax.rem(lax.div(z, 2), 2), lax.rem(z, 2)
    v = apply_map(v, table[3 * za], unit)
    v = apply_map(v, table[zb * (1 + za)], unit)
    v = apply_map(v, gath[zc * (z - 1) + (1 - zc) * NZ], unit)
    enter = column(v, unit)

    half = S // 2

    def feat_copy(q, part, who):
        return pltpu.make_async_remote_copy(
            src_ref=feats.at[head, pl.ds(part * half, half)],
            dst_ref=feats.at[who, pl.ds(part * half, half)],
            send_sem=f_send.at[part, q[0] * 2 + q[1]],
            recv_sem=f_recv.at[part, q[0] * 2 + q[1]],
            device_id=at_head(peer(q)),
            device_id_type=MESH,
        )

    for b in range(NB):
        e = jnp.sum(enter * bpre[b, 0:S, :], axis=0, keepdims=True) + bpre[b, S : S + 1, :]
        e = jnp.broadcast_to(column(e, unit), (S, S))
        rows = [
            jnp.sum(e * pre_maps[b * L + step], axis=0, keepdims=True) + shifts[step, b : b + 1, :]
            for step in range(L)
        ]
        out = jnp.concatenate(rows, axis=0)
        states_out[b * L : (b + 1) * L, :] = out
        feats[head, b * L : (b + 1) * L, :] = out.astype(BF16)
        if b % (NB // 2) == NB // 2 - 1:
            for q in peers:
                feat_copy(q, b // (NB // 2), head).start()

    def of_chip(dx, rows):
        chip = lax.rem(x + nx - dx, nx)
        both = jnp.concatenate([feats[2 * chip, rows], feats[2 * chip + 1, rows]], axis=1)
        return both, pl.ds(pl.multiple_of(chip * 2 * S, 2 * S), 2 * S)

    ring_dx = [0, 1, nx - 1, 2]
    for part in range(2):
        rows = slice(part * half, (part + 1) * half)
        pre = jnp.zeros((half, w_up.shape[1]), F32)
        for dx in ring_dx:
            for q in ((dx, 1), (dx, 0)):
                if q != (0, 0):
                    feat_copy(q, part, back(q)).wait_recv()
            both, cols = of_chip(dx, rows)
            pre = pre + jnp.dot(both, w_up[cols, :], preferred_element_type=F32)
        gate = jax.nn.sigmoid(pre)
        hidden[rows, :] = (pre * gate).astype(BF16)
        pgrad[rows, :] = (hgrad[rows, :] * gate * (1.0 + pre * (1.0 - gate))).astype(BF16)

    rows = S * nhead // ny
    share = rows // NZ
    for i in range(ny):
        out = jnp.dot(ctrans[pl.ds(i * rows, rows), :], hidden[...], preferred_element_type=F32).astype(BF16)
        place = lax.rem(i - y + ny, ny)
        piece = sum(jnp.where(place == t, n, 0) for n, t in enumerate(TURN))
        for j in range(NZ):
            dblk[j, pl.ds(pl.multiple_of(piece * share, share), share)] = out[j * share : (j + 1) * share]
    ring_b1 = Ring(NZ, z, along_z, dblk, lb1, b1s, b1r)
    ring_b1.begin()
    for dx in ring_dx:
        both, cols = of_chip(dx, slice(0, S))
        ftrans[cols, :] = both.astype(F32).T.astype(BF16)
    for i in range(ny):
        out = jnp.dot(ftrans[pl.ds(i * rows, rows), :], pgrad[...], preferred_element_type=F32).astype(BF16)
        for j in range(NZ):
            place = lax.rem(j - z + NZ, NZ)
            piece = sum(jnp.where(place == t, n, 0) for n, t in enumerate(ORDER))
            ublk[i, pl.ds(pl.multiple_of(piece * share, share), share)] = out[j * share : (j + 1) * share]
    ring_a1 = Ring(ny, y, along_y, ublk, la1, a1s, a1r)
    ring_a1.begin()

    for h in range(nhead):
        parts[h, 0] = dot_t(hidden[...], w_down[pl.ds(h * S, S), :]).astype(BF16)
        parts[h, 1] = dot_t(pgrad[...], w_up[pl.ds(h * S, S), :]).astype(BF16)
    for q in peers:
        head_copy(q, parts.at[peer(q)], landed.at[head], o_send, o_recv).start()

    def up_copy(r):
        return pltpu.make_async_remote_copy(
            src_ref=u2blk.at[r],
            dst_ref=la2.at[r],
            send_sem=a2s.at[r],
            recv_sem=a2r.at[r],
            device_id=along_z(lax.rem(z + r, NZ)),
            device_id_type=MESH,
        )

    def up_part(c):
        out = ring_a1.total(c)
        for i in range(2):
            r = ORDER[2 * c + i]
            mine = out[i * share : (i + 1) * share]
            if r == 0:
                gup_out[...] = mine
            else:
                u2blk[r] = mine.astype(BF16)
                up_copy(r).start()

    def down_copy(r):
        return pltpu.make_async_remote_copy(
            src_ref=d2blk.at[r],
            dst_ref=lb2.at[r],
            send_sem=b2s.at[r],
            recv_sem=b2r.at[r],
            device_id=along_y(lax.rem(y + r, ny)),
            device_id_type=MESH,
        )

    def down_part(c):
        out = ring_b1.total(c)
        r = TURN[c]
        if r == 0:
            gdown_out[...] = out
        else:
            d2blk[r] = out.astype(BF16)
            down_copy(r).start()

    ring_b1.advance(0, False)
    ring_a1.advance(0, False)
    ring_b1.advance(1, True)
    ring_b1.advance(1, False)
    ring_b1.advance(2, True)
    ring_b1.advance(2, False)
    for q in peers:
        head_copy(q, parts.at[peer(q)], landed.at[back(q)], o_send, o_recv).wait_recv()
    outs = [parts[head, i].astype(F32) for i in range(2)]
    for q in peers:
        outs = [outs[i] + landed[back(q), i].astype(F32) for i in range(2)]
    mlp_out[...] = outs[0].astype(BF16)
    sgrad_out[...] = outs[1].astype(BF16)
    up_part(0)
    up_part(2)
    up_part(1)
    up_part(3)
    for c in (0, 2, 1, 3):
        down_part(c)
    for r in (1, 7, 2, 6, 3, 5, 4):
        up_copy(r).wait_recv()
        gup_out[...] += la2[r].astype(F32)
    for r in (1, 3, 2):
        down_copy(r).wait_recv()
        gdown_out[...] += lb2[r].astype(F32)

    row_copy.wait_send()
    for q in peers:
        head_copy(q, cot, cots.at[head], c_send, c_recv).wait_send()
        for part in range(2):
            feat_copy(q, part, head).wait_send()
        head_copy(q, parts.at[peer(q)], landed.at[head], o_send, o_recv).wait_send()
    for n in range(8):
        for c in legs(n):
            leg(n, c).wait_send()

    @pl.when(y == 0)
    def _():
        for row in range(1, ny):
            tell_state(row).wait_send()

    for owner in range(1, ny - 1):

        @pl.when(y == owner)
        def _():
            for row in range(owner + 1, ny):
                tell_map(row, owner).wait_send()

    for ring in (ring_a1, ring_b1):
        ring.finish()
    for r in range(1, NZ):
        up_copy(r).wait_send()
    for r in range(1, ny):
        down_copy(r).wait_send()


def settle(*refs):
    for src, dst in zip(refs[:5], refs[5:]):
        dst[...] = src[...]


def on_device(ntok, nhead, guess, drive, decay, mixing, init_state, skew_gen, w_up, w_down, cotangent):
    ny = ntok // NZ
    width, ff = w_up.shape
    share = width // ntok
    vm = pl.BlockSpec(memory_space=pltpu.VMEM)
    dma = pltpu.SemaphoreType.DMA
    landing = lambda n, rows: pltpu.VMEM((2, n // 2, PIECES, rows // PIECES, ff), BF16)
    sems = lambda n: dma((2, n // 2, PIECES))
    scratch = [
        pltpu.VMEM((width, ff), BF16),
        pltpu.VMEM((width, ff), BF16),
        dma((2,)),
        pltpu.VMEM((S + 8, S), F32),
        dma,
        dma,
        pltpu.VMEM((2 * S, 2 * S), BF16),
        pltpu.VMEM((S, S), F32),
        pltpu.VMEM((S, S), F32),
        pltpu.VMEM((S, S, S), F32),
        pltpu.VMEM((L, NB, S), F32),
        pltpu.VMEM((4, MR, S), F32),
        pltpu.VMEM((NB, MR, S), F32),
        pltpu.VMEM((NZ + 1, MR, S), F32),
        dma((len(LEGS), len(CUTS))),
        dma((len(LEGS), len(CUTS))),
        pltpu.VMEM((4, MR, S), F32),
        pltpu.VMEM((8, S), F32),
        pltpu.VMEM((8, S), F32),
        pltpu.VMEM((ny - 2, MR, S), F32),
        pltpu.VMEM((MR, S), F32),
        dma((ny,)),
        dma((ny - 1,)),
        pltpu.VMEM((nhead, S, S), BF16),
        dma((2, nhead)),
        dma((2, nhead)),
        pltpu.VMEM((nhead, S, S), BF16),
        dma((nhead,)),
        dma((nhead,)),
        pltpu.VMEM((S, ff), F32),
        pltpu.VMEM((S, ff), BF16),
        pltpu.VMEM((S, ff), BF16),
        pltpu.VMEM((width, S), BF16),
        pltpu.VMEM((width, S), BF16),
        pltpu.VMEM((nhead, 2, S, S), BF16),
        pltpu.VMEM((nhead, 2, S, S), BF16),
        dma((nhead,)),
        dma((nhead,)),
        pltpu.VMEM((ny, NZ * share, ff), BF16),
        pltpu.VMEM((NZ, ny * share, ff), BF16),
        pltpu.VMEM((NZ, share, ff), BF16),
        pltpu.VMEM((ny, share, ff), BF16),
        landing(ny, NZ * share),
        pltpu.VMEM((NZ, share, ff), BF16),
        landing(NZ, ny * share),
        pltpu.VMEM((ny, share, ff), BF16),
        sems(ny),
        sems(ny),
        dma((NZ,)),
        dma((NZ,)),
        sems(NZ),
        sems(NZ),
        dma((ny,)),
        dma((ny,)),
    ]
    results = [((S, S), F32), ((S, S), BF16), ((S, S), BF16), ((share, ff), F32), ((share, ff), F32)]
    done = pl.pallas_call(
        functools.partial(kernel, ntok, nhead),
        out_shape=tuple(pltpu.VMEM(*r) for r in results),
        in_specs=[vm] * 6 + [pl.BlockSpec(memory_space=pl.ANY)] * 2 + [vm],
        out_specs=[vm] * 5,
        scratch_shapes=scratch,
        compiler_params=pltpu.CompilerParams(
            collective_id=0, has_side_effects=True, vmem_limit_bytes=56 * 1024 * 1024
        ),
    )(
        guess,
        drive,
        decay,
        mixing.reshape(1, S),
        init_state.reshape(1, S),
        skew_gen.reshape(S, S),
        w_up,
        w_down,
        cotangent,
    )
    return pl.pallas_call(
        settle,
        out_shape=tuple(jax.ShapeDtypeStruct(*r) for r in results),
        in_specs=[vm] * 5,
        out_specs=[vm] * 5,
    )(*[pltpu.with_memory_space_constraint(d, pltpu.VMEM) for d in done])


def solution(mesh):
    placed = (
        P("tok", "head"),
        P("tok", "head"),
        P("tok", "head"),
        P("head"),
        P("head"),
        P("head", None, None),
        P(None, "head"),
        P(None, "head"),
        P("tok", "head"),
    )
    return jax.shard_map(
        functools.partial(on_device, mesh.shape["tok"], mesh.shape["head"]),
        mesh=mesh,
        in_specs=placed,
        out_specs=(P("tok", "head"),) * 5,
        check_vma=False,
    )
```

```python
import functools

import jax
import jax.numpy as jnp
from jax import lax
from jax.experimental import pallas as pl
from jax.experimental.pallas import tpu as pltpu
from jax.sharding import PartitionSpec as P

MESH = pl.DeviceIdType.MESH
F32, BF16 = jnp.float32, jnp.bfloat16
S = 128
NZ = 8
NB, L = 8, 16
MR = 144
SPREAD = 86.0
NEWTON = 11
LEGS = (4, 3, 5, 2, 6, 1, 7)
PIECES = 4
ORDER = (4, 3, 6, 1, 5, 2, 7, 0)
TURN = (2, 3, 1, 0)


def split(x):
    hi = x.astype(BF16)
    return hi, (x - hi.astype(F32)).astype(BF16)


def left(x):
    return jnp.concatenate(split(x), axis=1)


def right(x):
    both = jnp.concatenate(split(x), axis=1)
    return jnp.concatenate([both, both], axis=0)


def product(l, r):
    out = jnp.dot(l, r, preferred_element_type=F32)
    return out[:, :S] + out[:, S:]


def mm(a, b):
    return product(left(a), right(b))


def compose(first, then):
    out = mm(first, then[:S])
    return jnp.concatenate([out[:S], out[S:] + then[S:]], axis=0)


def eye():
    rows = lax.broadcasted_iota(jnp.int32, (S, S), 0)
    cols = lax.broadcasted_iota(jnp.int32, (S, S), 1)
    return jnp.where(rows == cols, 1.0, 0.0).astype(F32)


def column(v, unit):
    return jnp.sum(unit * v, axis=1, keepdims=True)


def apply_map(v, m, unit):
    return jnp.sum(column(v, unit) * m[:S], axis=0, keepdims=True) + m[S : S + 1]


def dot_t(a, b):
    return lax.dot_general(a, b, (((1,), (1,)), ((), ())), preferred_element_type=F32)


def encode(matrix, shift):
    high, rest = split(shift)
    low = (shift - high.astype(F32) - rest.astype(F32)).astype(BF16)
    rows = [high[:1], rest[:1], low[:1], high[1:14]]
    matrix = jnp.exp(jnp.clip(matrix, -1.01, 1.01) * SPREAD).astype(BF16)
    return jnp.concatenate([matrix, jnp.concatenate([r.astype(F32) for r in rows], axis=0).astype(BF16)], axis=0)


def decode(ref, at):
    matrix = jnp.log(ref[at, 0:S, :].astype(F32)) * (1.0 / SPREAD)
    tail = ref[at, S:MR, :].astype(F32)
    shift = tail[0:1] + tail[1:2] + tail[2:3]
    return jnp.concatenate([matrix, shift, jnp.zeros((MR - S - 1, S), F32)], axis=0)


class Ring:
    def __init__(self, n, me, device, blocks, landing, send, recv):
        self.n, self.me, self.device = n, me, device
        self.blocks, self.landing, self.send, self.recv = blocks, landing, send, recv
        self.rows = blocks.shape[1] // PIECES

    def owner(self, d, hop):
        way = 1 if d == 0 else -1
        return lax.rem(self.me + way * (self.n // 2 - hop) + 2 * self.n, self.n)

    def at(self, c):
        return pl.ds(c * self.rows, self.rows)

    def copy(self, d, hop, c):
        target = lax.rem(self.me + (1 if d == 0 else -1) + self.n, self.n)
        return pltpu.make_async_remote_copy(
            src_ref=self.blocks.at[self.owner(d, hop), self.at(c)],
            dst_ref=self.landing.at[d, hop, c],
            send_sem=self.send.at[d, hop, c],
            recv_sem=self.recv.at[d, hop, c],
            device_id=self.device(target),
            device_id_type=MESH,
        )

    @staticmethod
    def first(d):
        return (0, 1) if d == 0 else (2, 3)

    def begin(self):
        for i in range(2):
            for d in range(2):
                self.copy(d, 0, self.first(d)[i]).start()
        for i in range(2):
            for d in range(2):
                self.copy(d, 1, self.first(1 - d)[i]).start()

    def advance(self, hop, early):
        for i in range(2):
            for d in range(2):
                c = self.first(1 - d if early else d)[i]
                self.copy(d, hop, c).wait_recv()
                to = self.owner(d, hop + 1)
                self.blocks[to, self.at(c)] = (
                    self.blocks[to, self.at(c)].astype(F32) + self.landing[d, hop, c].astype(F32)
                ).astype(BF16)
                self.copy(d, hop + 1, c).start()

    def total(self, c):
        last = self.n // 2 - 1
        out = self.blocks[self.me, self.at(c)].astype(F32)
        for d in range(2):
            self.copy(d, last, c).wait_recv()
            out = out + self.landing[d, last, c].astype(F32)
        return out

    def finish(self):
        for hop in range(self.n // 2):
            for d in range(2):
                for c in self.first(d) if hop == 0 else range(PIECES):
                    self.copy(d, hop, c).wait_send()


def kernel(
    ntok,
    nhead,
    guess,
    drive,
    decay,
    mixing,
    init,
    skew,
    w_up_hbm,
    w_down_hbm,
    cot,
    states_out,
    mlp_out,
    sgrad_out,
    gup_out,
    gdown_out,
    w_up,
    w_down,
    w_sem,
    shifted,
    behind,
    row_send,
    row_recv,
    wrot,
    slopes,
    offs,
    pre_maps,
    shifts,
    bmaps,
    bpre,
    gath,
    coded,
    gsend,
    grecv,
    table,
    vin,
    vout,
    tin,
    tout,
    v_send,
    v_recv,
    feats,
    f_send,
    f_recv,
    cots,
    c_send,
    c_recv,
    hgrad,
    hidden,
    pgrad,
    ftrans,
    ctrans,
    parts,
    landed,
    o_send,
    o_recv,
    ublk,
    dblk,
    u2blk,
    d2blk,
    la1,
    la2,
    lb1,
    lb2,
    a1s,
    a1r,
    a2s,
    a2r,
    b1s,
    b1r,
    b2s,
    b2r,
):
    ny, nx = ntok // NZ, nhead // 2
    tok, head = lax.axis_index("tok"), lax.axis_index("head")
    y, z = lax.div(tok, NZ), lax.rem(tok, NZ)
    x, core = lax.div(head, 2), lax.rem(head, 2)

    def along_z(target):
        return {"tok": y * NZ + target, "head": head}

    def along_y(target):
        return {"tok": target * NZ + z, "head": head}

    def at_tok(target):
        return {"tok": target, "head": head}

    def at_head(target):
        return {"tok": tok, "head": target}

    peers = [(dx, flip) for dx in ([0, 1, nx - 1, 2] if nx >= 4 else range(nx)) for flip in (1, 0)]
    peers = [q for q in peers if q != (0, 0)]

    def peer(q):
        return lax.rem(x + q[0], nx) * 2 + lax.rem(core + q[1], 2)

    after, before_me = lax.rem(tok + 1, ntok), lax.rem(tok + ntok - 1, ntok)

    barrier = pltpu.get_barrier_semaphore()
    greet = [along_z(lax.rem(z + i, NZ)) for i in range(1, NZ)]
    greet += [along_y(lax.rem(y + i, ny)) for i in range(1, ny)]
    greet += [at_tok(after), at_tok(before_me)]
    greet += [at_head(peer(q)) for q in peers]
    for who in greet:
        pl.semaphore_signal(barrier, inc=1, device_id=who, device_id_type=MESH)
    loads = [
        pltpu.make_async_copy(w_up_hbm, w_up, w_sem.at[0]),
        pltpu.make_async_copy(w_down_hbm, w_down, w_sem.at[1]),
    ]
    for load in loads:
        load.start()

    unit = eye()
    k = skew[...]
    a = unit + k
    kk = mm(k, k)
    bound = jnp.sqrt(jnp.sum(jnp.sum(kk * kk, axis=1, keepdims=True), axis=0, keepdims=True) * 0.5)
    top = 1.0 + 1.01 * bound
    scale = 2.0 / (1.0 + top)
    gap = (top - 1.0) / (top + 1.0)

    def newton(v, t, gap):
        square = gap * gap
        wide = 2.0 / (2.0 - square)
        out = product(left(jnp.concatenate([t, v], axis=0)), right(wide * (2.0 * unit - t)))
        return out[S:], out[:S], square / (2.0 - square)

    v, t = (unit - k) * scale, (unit - kk) * scale
    for _ in range(NEWTON // 2):
        v, t, gap = newton(v, t, gap)

    pl.semaphore_wait(barrier, len(greet))
    row_copy = pltpu.make_async_remote_copy(
        src_ref=guess.at[pl.ds(S - 8, 8)],
        dst_ref=behind,
        send_sem=row_send,
        recv_sem=row_recv,
        device_id=at_tok(after),
        device_id_type=MESH,
    )
    row_copy.start()

    def head_copy(q, src, dst, send, recv):
        return pltpu.make_async_remote_copy(
            src_ref=src,
            dst_ref=dst,
            send_sem=send.at[q[0] * 2 + q[1]],
            recv_sem=recv.at[q[0] * 2 + q[1]],
            device_id=at_head(peer(q)),
            device_id_type=MESH,
        )

    def back(q):
        return lax.rem(x + nx - q[0], nx) * 2 + lax.rem(core + q[1], 2)

    for q in peers:
        head_copy(q, cot, cots.at[head], c_send, c_recv).start()
    cots[head] = cot[...]

    for _ in range(NEWTON - NEWTON // 2):
        v, t, gap = newton(v, t, gap)
    t = jnp.dot(a, v, precision=lax.Precision.HIGHEST, preferred_element_type=F32)
    v = v + mm(v, unit - t)
    rot_t = 2.0 * v - unit
    wrot[...] = right(rot_t)

    m = mixing[...]

    def tangent(before, decay):
        bent = jnp.tanh(before)
        curve = 1.0 - bent * bent
        return (1.0 - m) * decay + m * curve, m * (bent - curve * before)

    shifted[pl.ds(8, S), :] = guess[...]
    first = lax.broadcasted_iota(jnp.int32, (S, S), 0) == 0
    slope, push = tangent(jnp.where(first, 0.0, shifted[pl.ds(7, S), :]), decay[...])
    slopes[...] = jnp.where(first, 1.0, slope)
    offs[...] = product(left(jnp.where(first, 0.0, push)), wrot[...]) + drive[...]

    def advance(step, blocks, shift):
        rows = [left(blocks[b] * slopes[pl.ds(b * L + step, 1), :]) for b in range(NB)]
        shift = shift * slopes[pl.ds(step, NB, stride=L), :]
        rows.append(left(jnp.concatenate([shift, jnp.zeros((16 - NB, S), F32)], axis=0)))
        out = product(jnp.concatenate(rows, axis=0), wrot[...])
        for b in range(NB):
            pre_maps[b * L + step] = out[b * S : (b + 1) * S]
        shifts[step] = out[NB * S : NB * S + NB] + offs[pl.ds(step, NB, stride=L), :]

    advance(0, [unit] * NB, jnp.zeros((NB, S), F32))

    for step in range(1, L):
        advance(step, [pre_maps[b * L + step - 1] for b in range(NB)], shifts[step - 1])

    pad = jnp.zeros((MR - S - 1, S), F32)

    def block_map(b):
        return jnp.concatenate([pre_maps[b * L + L - 1], shifts[L - 1, b : b + 1], pad], axis=0)

    none = jnp.concatenate([unit, jnp.zeros((MR - S, S), F32)], axis=0)
    bpre[0] = none
    bpre[1] = block_map(0)
    bpre[2] = compose(block_map(0), block_map(1))
    bmaps[0] = compose(block_map(2), block_map(3))
    bmaps[1] = compose(block_map(4), block_map(5))
    bmaps[2] = compose(block_map(6), block_map(7))
    bpre[4] = compose(bpre[2], bmaps[0])
    bmaps[3] = compose(bmaps[1], bmaps[2])
    own = compose(bpre[4], bmaps[3])
    row_copy.wait_recv()
    first_slope, first_push = tangent(jnp.where(tok == 0, init[...], behind[7:8, :]), decay[0:1, :])
    own_shift = jnp.concatenate([apply_map(first_push, own, unit), jnp.zeros((MR - S - 1, S), F32)], axis=0)
    own = column(first_slope, unit) * own[:S]
    gath[z] = jnp.concatenate([own, own_shift], axis=0)
    coded[z] = encode(own, own_shift)

    def leg(r, owner):
        return pltpu.make_async_remote_copy(
            src_ref=coded.at[owner],
            dst_ref=coded.at[owner],
            send_sem=gsend.at[r],
            recv_sem=grecv.at[r],
            device_id=along_z(lax.rem(z + r, NZ)),
            device_id_type=MESH,
        )

    for r in LEGS:
        leg(r, z).start()

    for load in loads:
        load.wait()
    for q in peers:
        head_copy(q, cot, cots.at[back(q)], c_send, c_recv).wait_recv()
    hgrad[...] = jnp.zeros_like(hgrad)
    for c in range(nx):
        hgrad[...] += jnp.dot(
            jnp.concatenate([cots[2 * c], cots[2 * c + 1]], axis=1),
            w_down[pl.ds(c * 2 * S, 2 * S), :],
            preferred_element_type=F32,
        )
    for h in range(nhead):
        ctrans[pl.ds(h * S, S), :] = cots[h].astype(F32).T.astype(BF16)
    bpre[3] = compose(bpre[2], block_map(2))
    bpre[5] = compose(bpre[4], block_map(4))
    bpre[6] = compose(bpre[4], bmaps[1])
    bpre[7] = compose(bpre[6], block_map(6))
    gath[NZ] = none
    table[0] = none
    for r in (1, 7, 2, 6, 3, 5, 4):
        owner = lax.rem(z - r + NZ, NZ)
        leg(r, owner).wait_recv()
        gath[owner] = decode(coded, owner)
    pairs = [compose(gath[2 * i], gath[2 * i + 1]) for i in range(4)]
    table[1] = pairs[0]
    table[2] = pairs[2]
    low = compose(pairs[0], pairs[1])
    table[3] = low
    whole = compose(low, compose(pairs[2], pairs[3]))

    def tell_state(row):
        return pltpu.make_async_remote_copy(
            src_ref=vout,
            dst_ref=vin,
            send_sem=v_send.at[row],
            recv_sem=v_recv.at[0],
            device_id=along_y(row),
            device_id_type=MESH,
        )

    def tell_map(row, owner):
        return pltpu.make_async_remote_copy(
            src_ref=tout,
            dst_ref=tin.at[owner - 1],
            send_sem=v_send.at[row],
            recv_sem=v_recv.at[owner],
            device_id=along_y(row),
            device_id_type=MESH,
        )

    @pl.when(y == 0)
    def _():
        vout[...] = jnp.broadcast_to(apply_map(init[...], whole, unit), (8, S))
        for row in range(ny - 1, 0, -1):
            tell_state(row).start()
        vin[...] = jnp.broadcast_to(init[...], (8, S))

    for owner in range(1, ny - 1):

        @pl.when(y == owner)
        def _():
            tout[...] = encode(whole[:S], whole[S:])
            for row in range(ny - 1, owner, -1):
                tell_map(row, owner).start()

    @pl.when(y > 0)
    def _():
        tell_state(1).wait_recv()

    for owner in range(1, ny - 1):

        @pl.when(y > owner)
        def _():
            tell_map(ny - 1, owner).wait_recv()
            vin[...] = jnp.broadcast_to(apply_map(vin[0:1, :], decode(tin, owner - 1), unit), (8, S))

    v = vin[0:1, :]
    za, zb, zc = lax.div(z, 4), lax.rem(lax.div(z, 2), 2), lax.rem(z, 2)
    v = apply_map(v, table[3 * za], unit)
    v = apply_map(v, table[zb * (1 + za)], unit)
    v = apply_map(v, gath[zc * (z - 1) + (1 - zc) * NZ], unit)
    enter = column(v * first_slope + first_push, unit)

    half = S // 2

    def feat_copy(q, part, who):
        return pltpu.make_async_remote_copy(
            src_ref=feats.at[head, pl.ds(part * half, half)],
            dst_ref=feats.at[who, pl.ds(part * half, half)],
            send_sem=f_send.at[part, q[0] * 2 + q[1]],
            recv_sem=f_recv.at[part, q[0] * 2 + q[1]],
            device_id=at_head(peer(q)),
            device_id_type=MESH,
        )

    for b in range(NB):
        e = jnp.sum(enter * bpre[b, 0:S, :], axis=0, keepdims=True) + bpre[b, S : S + 1, :]
        e = jnp.broadcast_to(column(e, unit), (S, S))
        rows = [
            jnp.sum(e * pre_maps[b * L + step], axis=0, keepdims=True) + shifts[step, b : b + 1, :]
            for step in range(L)
        ]
        out = jnp.concatenate(rows, axis=0)
        states_out[b * L : (b + 1) * L, :] = out
        feats[head, b * L : (b + 1) * L, :] = out.astype(BF16)
        if b % (NB // 2) == NB // 2 - 1:
            for q in peers:
                feat_copy(q, b // (NB // 2), head).start()

    def of_chip(dx, rows):
        chip = lax.rem(x + nx - dx, nx)
        both = jnp.concatenate([feats[2 * chip, rows], feats[2 * chip + 1, rows]], axis=1)
        return both, pl.ds(pl.multiple_of(chip * 2 * S, 2 * S), 2 * S)

    ring_dx = [0, 1, nx - 1, 2]
    for part in range(2):
        rows = slice(part * half, (part + 1) * half)
        pre = jnp.zeros((half, w_up.shape[1]), F32)
        for dx in ring_dx:
            for q in ((dx, 1), (dx, 0)):
                if q != (0, 0):
                    feat_copy(q, part, back(q)).wait_recv()
            both, cols = of_chip(dx, rows)
            pre = pre + jnp.dot(both, w_up[cols, :], preferred_element_type=F32)
        gate = jax.nn.sigmoid(pre)
        hidden[rows, :] = (pre * gate).astype(BF16)
        pgrad[rows, :] = (hgrad[rows, :] * gate * (1.0 + pre * (1.0 - gate))).astype(BF16)

    rows = S * nhead // ny
    share = rows // NZ
    for i in range(ny):
        out = jnp.dot(ctrans[pl.ds(i * rows, rows), :], hidden[...], preferred_element_type=F32).astype(BF16)
        place = lax.rem(i - y + ny, ny)
        piece = sum(jnp.where(place == t, n, 0) for n, t in enumerate(TURN))
        for j in range(NZ):
            dblk[j, pl.ds(pl.multiple_of(piece * share, share), share)] = out[j * share : (j + 1) * share]
    ring_b1 = Ring(NZ, z, along_z, dblk, lb1, b1s, b1r)
    ring_b1.begin()
    for dx in ring_dx:
        both, cols = of_chip(dx, slice(0, S))
        ftrans[cols, :] = both.astype(F32).T.astype(BF16)
    for i in range(ny):
        out = jnp.dot(ftrans[pl.ds(i * rows, rows), :], pgrad[...], preferred_element_type=F32).astype(BF16)
        for j in range(NZ):
            place = lax.rem(j - z + NZ, NZ)
            piece = sum(jnp.where(place == t, n, 0) for n, t in enumerate(ORDER))
            ublk[i, pl.ds(pl.multiple_of(piece * share, share), share)] = out[j * share : (j + 1) * share]
    ring_a1 = Ring(ny, y, along_y, ublk, la1, a1s, a1r)
    ring_a1.begin()

    for h in range(nhead):
        parts[h, 0] = dot_t(hidden[...], w_down[pl.ds(h * S, S), :]).astype(BF16)
        parts[h, 1] = dot_t(pgrad[...], w_up[pl.ds(h * S, S), :]).astype(BF16)
    for q in peers:
        head_copy(q, parts.at[peer(q)], landed.at[head], o_send, o_recv).start()

    def up_copy(r):
        return pltpu.make_async_remote_copy(
            src_ref=u2blk.at[r],
            dst_ref=la2.at[r],
            send_sem=a2s.at[r],
            recv_sem=a2r.at[r],
            device_id=along_z(lax.rem(z + r, NZ)),
            device_id_type=MESH,
        )

    def up_part(c):
        out = ring_a1.total(c)
        for i in range(2):
            r = ORDER[2 * c + i]
            mine = out[i * share : (i + 1) * share]
            if r == 0:
                gup_out[...] = mine
            else:
                u2blk[r] = mine.astype(BF16)
                up_copy(r).start()

    def down_copy(r):
        return pltpu.make_async_remote_copy(
            src_ref=d2blk.at[r],
            dst_ref=lb2.at[r],
            send_sem=b2s.at[r],
            recv_sem=b2r.at[r],
            device_id=along_y(lax.rem(y + r, ny)),
            device_id_type=MESH,
        )

    def down_part(c):
        out = ring_b1.total(c)
        r = TURN[c]
        if r == 0:
            gdown_out[...] = out
        else:
            d2blk[r] = out.astype(BF16)
            down_copy(r).start()

    ring_b1.advance(0, False)
    ring_a1.advance(0, False)
    ring_b1.advance(1, True)
    ring_b1.advance(1, False)
    ring_b1.advance(2, True)
    ring_b1.advance(2, False)
    for q in peers:
        head_copy(q, parts.at[peer(q)], landed.at[back(q)], o_send, o_recv).wait_recv()
    outs = [parts[head, i].astype(F32) for i in range(2)]
    for q in peers:
        outs = [outs[i] + landed[back(q), i].astype(F32) for i in range(2)]
    mlp_out[...] = outs[0].astype(BF16)
    sgrad_out[...] = outs[1].astype(BF16)
    up_part(0)
    up_part(2)
    up_part(1)
    up_part(3)
    for c in (0, 2, 1, 3):
        down_part(c)
    for r in (1, 7, 2, 6, 3, 5, 4):
        up_copy(r).wait_recv()
        gup_out[...] += la2[r].astype(F32)
    for r in (1, 3, 2):
        down_copy(r).wait_recv()
        gdown_out[...] += lb2[r].astype(F32)

    row_copy.wait_send()
    for q in peers:
        head_copy(q, cot, cots.at[head], c_send, c_recv).wait_send()
        for part in range(2):
            feat_copy(q, part, head).wait_send()
        head_copy(q, parts.at[peer(q)], landed.at[head], o_send, o_recv).wait_send()
    for r in LEGS:
        leg(r, z).wait_send()

    @pl.when(y == 0)
    def _():
        for row in range(1, ny):
            tell_state(row).wait_send()

    for owner in range(1, ny - 1):

        @pl.when(y == owner)
        def _():
            for row in range(owner + 1, ny):
                tell_map(row, owner).wait_send()

    for ring in (ring_a1, ring_b1):
        ring.finish()
    for r in range(1, NZ):
        up_copy(r).wait_send()
    for r in range(1, ny):
        down_copy(r).wait_send()


def settle(*refs):
    for src, dst in zip(refs[:5], refs[5:]):
        dst[...] = src[...]


def on_device(ntok, nhead, guess, drive, decay, mixing, init_state, skew_gen, w_up, w_down, cotangent):
    ny = ntok // NZ
    width, ff = w_up.shape
    share = width // ntok
    vm = pl.BlockSpec(memory_space=pltpu.VMEM)
    dma = pltpu.SemaphoreType.DMA
    landing = lambda n, rows: pltpu.VMEM((2, n // 2, PIECES, rows // PIECES, ff), BF16)
    sems = lambda n: dma((2, n // 2, PIECES))
    scratch = [
        pltpu.VMEM((width, ff), BF16),
        pltpu.VMEM((width, ff), BF16),
        dma((2,)),
        pltpu.VMEM((S + 8, S), F32),
        pltpu.VMEM((8, S), F32),
        dma,
        dma,
        pltpu.VMEM((2 * S, 2 * S), BF16),
        pltpu.VMEM((S, S), F32),
        pltpu.VMEM((S, S), F32),
        pltpu.VMEM((S, S, S), F32),
        pltpu.VMEM((L, NB, S), F32),
        pltpu.VMEM((4, MR, S), F32),
        pltpu.VMEM((NB, MR, S), F32),
        pltpu.VMEM((NZ + 1, MR, S), F32),
        pltpu.VMEM((NZ, MR, S), BF16),
        dma((NZ,)),
        dma((NZ,)),
        pltpu.VMEM((4, MR, S), F32),
        pltpu.VMEM((8, S), F32),
        pltpu.VMEM((8, S), F32),
        pltpu.VMEM((ny - 2, MR, S), BF16),
        pltpu.VMEM((MR, S), BF16),
        dma((ny,)),
        dma((ny - 1,)),
        pltpu.VMEM((nhead, S, S), BF16),
        dma((2, nhead)),
        dma((2, nhead)),
        pltpu.VMEM((nhead, S, S), BF16),
        dma((nhead,)),
        dma((nhead,)),
        pltpu.VMEM((S, ff), F32),
        pltpu.VMEM((S, ff), BF16),
        pltpu.VMEM((S, ff), BF16),
        pltpu.VMEM((width, S), BF16),
        pltpu.VMEM((width, S), BF16),
        pltpu.VMEM((nhead, 2, S, S), BF16),
        pltpu.VMEM((nhead, 2, S, S), BF16),
        dma((nhead,)),
        dma((nhead,)),
        pltpu.VMEM((ny, NZ * share, ff), BF16),
        pltpu.VMEM((NZ, ny * share, ff), BF16),
        pltpu.VMEM((NZ, share, ff), BF16),
        pltpu.VMEM((ny, share, ff), BF16),
        landing(ny, NZ * share),
        pltpu.VMEM((NZ, share, ff), BF16),
        landing(NZ, ny * share),
        pltpu.VMEM((ny, share, ff), BF16),
        sems(ny),
        sems(ny),
        dma((NZ,)),
        dma((NZ,)),
        sems(NZ),
        sems(NZ),
        dma((ny,)),
        dma((ny,)),
    ]
    results = [((S, S), F32), ((S, S), BF16), ((S, S), BF16), ((share, ff), F32), ((share, ff), F32)]
    done = pl.pallas_call(
        functools.partial(kernel, ntok, nhead),
        out_shape=tuple(pltpu.VMEM(*r) for r in results),
        in_specs=[vm] * 6 + [pl.BlockSpec(memory_space=pl.ANY)] * 2 + [vm],
        out_specs=[vm] * 5,
        scratch_shapes=scratch,
        compiler_params=pltpu.CompilerParams(
            collective_id=0, has_side_effects=True, vmem_limit_bytes=56 * 1024 * 1024
        ),
    )(
        guess,
        drive,
        decay,
        mixing.reshape(1, S),
        init_state.reshape(1, S),
        skew_gen.reshape(S, S),
        w_up,
        w_down,
        cotangent,
    )
    return pl.pallas_call(
        settle,
        out_shape=tuple(jax.ShapeDtypeStruct(*r) for r in results),
        in_specs=[vm] * 5,
        out_specs=[vm] * 5,
    )(*[pltpu.with_memory_space_constraint(d, pltpu.VMEM) for d in done])


def solution(mesh):
    placed = (
        P("tok", "head"),
        P("tok", "head"),
        P("tok", "head"),
        P("head"),
        P("head"),
        P("head", None, None),
        P(None, "head"),
        P(None, "head"),
        P("tok", "head"),
    )
    return jax.shard_map(
        functools.partial(on_device, mesh.shape["tok"], mesh.shape["head"]),
        mesh=mesh,
        in_specs=placed,
        out_specs=(P("tok", "head"),) * 5,
        check_vma=False,
    )
```

```python
import functools

import jax
import jax.numpy as jnp
from jax import lax
from jax.experimental import pallas as pl
from jax.experimental.pallas import tpu as pltpu
from jax.sharding import PartitionSpec as P

MESH = pl.DeviceIdType.MESH
F32, BF16 = jnp.float32, jnp.bfloat16
S = 128
NZ = 8
NB, L = 8, 16
MR = 144
SPREAD = 86.0
NEWTON = 11
LEGS = (4, 3, 5, 2, 6, 1, 7)
PIECES = 4
ORDER = (4, 3, 6, 1, 5, 2, 7, 0)
TURN = (2, 3, 1, 0)


def split(x):
    hi = x.astype(BF16)
    return hi, (x - hi.astype(F32)).astype(BF16)


def left(x):
    return jnp.concatenate(split(x), axis=1)


def right(x):
    both = jnp.concatenate(split(x), axis=1)
    return jnp.concatenate([both, both], axis=0)


def product(l, r):
    out = jnp.dot(l, r, preferred_element_type=F32)
    return out[:, :S] + out[:, S:]


def mm(a, b):
    return product(left(a), right(b))


def compose(first, then):
    out = mm(first, then[:S])
    return jnp.concatenate([out[:S], out[S:] + then[S:]], axis=0)


def eye():
    rows = lax.broadcasted_iota(jnp.int32, (S, S), 0)
    cols = lax.broadcasted_iota(jnp.int32, (S, S), 1)
    return jnp.where(rows == cols, 1.0, 0.0).astype(F32)


def column(v, unit):
    return jnp.sum(unit * v, axis=1, keepdims=True)


def apply_map(v, m, unit):
    return jnp.sum(column(v, unit) * m[:S], axis=0, keepdims=True) + m[S : S + 1]


def dot_t(a, b):
    return lax.dot_general(a, b, (((1,), (1,)), ((), ())), preferred_element_type=F32)


def encode(matrix, shift):
    high, rest = split(shift)
    low = (shift - high.astype(F32) - rest.astype(F32)).astype(BF16)
    rows = [high[:1], rest[:1], low[:1], high[1:14]]
    matrix = jnp.exp(jnp.clip(matrix, -1.01, 1.01) * SPREAD).astype(BF16)
    return jnp.concatenate([matrix, jnp.concatenate([r.astype(F32) for r in rows], axis=0).astype(BF16)], axis=0)


def decode(ref, at):
    matrix = jnp.log(ref[at, 0:S, :].astype(F32)) * (1.0 / SPREAD)
    tail = ref[at, S:MR, :].astype(F32)
    shift = tail[0:1] + tail[1:2] + tail[2:3]
    return jnp.concatenate([matrix, shift, jnp.zeros((MR - S - 1, S), F32)], axis=0)


class Ring:
    def __init__(self, n, me, device, blocks, landing, send, recv):
        self.n, self.me, self.device = n, me, device
        self.blocks, self.landing, self.send, self.recv = blocks, landing, send, recv
        self.rows = blocks.shape[1] // PIECES

    def owner(self, d, hop):
        way = 1 if d == 0 else -1
        return lax.rem(self.me + way * (self.n // 2 - hop) + 2 * self.n, self.n)

    def at(self, c):
        return pl.ds(c * self.rows, self.rows)

    def copy(self, d, hop, c):
        target = lax.rem(self.me + (1 if d == 0 else -1) + self.n, self.n)
        return pltpu.make_async_remote_copy(
            src_ref=self.blocks.at[self.owner(d, hop), self.at(c)],
            dst_ref=self.landing.at[d, hop, c],
            send_sem=self.send.at[d, hop, c],
            recv_sem=self.recv.at[d, hop, c],
            device_id=self.device(target),
            device_id_type=MESH,
        )

    @staticmethod
    def first(d):
        return (0, 1) if d == 0 else (2, 3)

    def begin(self):
        for i in range(2):
            for d in range(2):
                self.copy(d, 0, self.first(d)[i]).start()
        for i in range(2):
            for d in range(2):
                self.copy(d, 1, self.first(1 - d)[i]).start()

    def advance(self, hop, early):
        for i in range(2):
            for d in range(2):
                c = self.first(1 - d if early else d)[i]
                self.copy(d, hop, c).wait_recv()
                to = self.owner(d, hop + 1)
                self.blocks[to, self.at(c)] = (
                    self.blocks[to, self.at(c)].astype(F32) + self.landing[d, hop, c].astype(F32)
                ).astype(BF16)
                self.copy(d, hop + 1, c).start()

    def total(self, c):
        last = self.n // 2 - 1
        out = self.blocks[self.me, self.at(c)].astype(F32)
        for d in range(2):
            self.copy(d, last, c).wait_recv()
            out = out + self.landing[d, last, c].astype(F32)
        return out

    def finish(self):
        for hop in range(self.n // 2):
            for d in range(2):
                for c in self.first(d) if hop == 0 else range(PIECES):
                    self.copy(d, hop, c).wait_send()


def kernel(
    ntok,
    nhead,
    guess,
    drive,
    decay,
    mixing,
    init,
    skew,
    w_up_hbm,
    w_down_hbm,
    cot,
    states_out,
    mlp_out,
    sgrad_out,
    gup_out,
    gdown_out,
    w_up,
    w_down,
    w_sem,
    shifted,
    behind,
    row_send,
    row_recv,
    wrot,
    slopes,
    offs,
    pre_maps,
    shifts,
    bmaps,
    bpre,
    gath,
    coded,
    gsend,
    grecv,
    table,
    vin,
    vout,
    tin,
    tout,
    v_send,
    v_recv,
    feats,
    f_send,
    f_recv,
    cots,
    c_send,
    c_recv,
    hgrad,
    hidden,
    pgrad,
    ftrans,
    ctrans,
    parts,
    landed,
    o_send,
    o_recv,
    ublk,
    dblk,
    u2blk,
    d2blk,
    la1,
    la2,
    lb1,
    lb2,
    a1s,
    a1r,
    a2s,
    a2r,
    b1s,
    b1r,
    b2s,
    b2r,
):
    ny, nx = ntok // NZ, nhead // 2
    tok, head = lax.axis_index("tok"), lax.axis_index("head")
    y, z = lax.div(tok, NZ), lax.rem(tok, NZ)
    x, core = lax.div(head, 2), lax.rem(head, 2)

    def along_z(target):
        return {"tok": y * NZ + target, "head": head}

    def along_y(target):
        return {"tok": target * NZ + z, "head": head}

    def at_tok(target):
        return {"tok": target, "head": head}

    def at_head(target):
        return {"tok": tok, "head": target}

    peers = [(dx, flip) for dx in ([0, 1, nx - 1, 2] if nx >= 4 else range(nx)) for flip in (1, 0)]
    peers = [q for q in peers if q != (0, 0)]

    def peer(q):
        return lax.rem(x + q[0], nx) * 2 + lax.rem(core + q[1], 2)

    after, before_me = lax.rem(tok + 1, ntok), lax.rem(tok + ntok - 1, ntok)

    barrier = pltpu.get_barrier_semaphore()
    greet = [along_z(lax.rem(z + i, NZ)) for i in range(1, NZ)]
    greet += [along_y(lax.rem(y + i, ny)) for i in range(1, ny)]
    greet += [at_tok(after), at_tok(before_me)]
    greet += [at_head(peer(q)) for q in peers]
    for who in greet:
        pl.semaphore_signal(barrier, inc=1, device_id=who, device_id_type=MESH)
    loads = [
        pltpu.make_async_copy(w_up_hbm, w_up, w_sem.at[0]),
        pltpu.make_async_copy(w_down_hbm, w_down, w_sem.at[1]),
    ]
    for load in loads:
        load.start()

    unit = eye()
    k = skew[...]
    a = unit + k
    kk = mm(k, k)
    bound = jnp.sqrt(jnp.sum(jnp.sum(kk * kk, axis=1, keepdims=True), axis=0, keepdims=True) * 0.5)
    top = 1.0 + 1.01 * bound
    scale = 2.0 / (1.0 + top)
    gap = (top - 1.0) / (top + 1.0)

    def newton(v, t, gap):
        square = gap * gap
        wide = 2.0 / (2.0 - square)
        out = product(left(jnp.concatenate([t, v], axis=0)), right(wide * (2.0 * unit - t)))
        return out[S:], out[:S], square / (2.0 - square)

    v, t = (unit - k) * scale, (unit - kk) * scale
    for _ in range(NEWTON):
        v, t, gap = newton(v, t, gap)
    t = jnp.dot(a, v, precision=lax.Precision.HIGHEST, preferred_element_type=F32)
    v = v + mm(v, unit - t)
    rot_t = 2.0 * v - unit
    wrot[...] = right(rot_t)

    pl.semaphore_wait(barrier, len(greet))
    row_copy = pltpu.make_async_remote_copy(
        src_ref=guess.at[pl.ds(S - 8, 8)],
        dst_ref=behind,
        send_sem=row_send,
        recv_sem=row_recv,
        device_id=at_tok(after),
        device_id_type=MESH,
    )
    row_copy.start()

    def head_copy(q, src, dst, send, recv):
        return pltpu.make_async_remote_copy(
            src_ref=src,
            dst_ref=dst,
            send_sem=send.at[q[0] * 2 + q[1]],
            recv_sem=recv.at[q[0] * 2 + q[1]],
            device_id=at_head(peer(q)),
            device_id_type=MESH,
        )

    def back(q):
        return lax.rem(x + nx - q[0], nx) * 2 + lax.rem(core + q[1], 2)

    for q in peers:
        head_copy(q, cot, cots.at[head], c_send, c_recv).start()
    cots[head] = cot[...]

    m = mixing[...]

    def tangent(before, decay):
        bent = jnp.tanh(before)
        curve = 1.0 - bent * bent
        return (1.0 - m) * decay + m * curve, m * (bent - curve * before)

    shifted[pl.ds(8, S), :] = guess[...]
    first = lax.broadcasted_iota(jnp.int32, (S, S), 0) == 0
    slope, push = tangent(jnp.where(first, 0.0, shifted[pl.ds(7, S), :]), decay[...])
    slopes[...] = jnp.where(first, 1.0, slope)
    offs[...] = product(left(jnp.where(first, 0.0, push)), wrot[...]) + drive[...]

    def advance(step, blocks, shift):
        rows = [left(blocks[b] * slopes[pl.ds(b * L + step, 1), :]) for b in range(NB)]
        shift = shift * slopes[pl.ds(step, NB, stride=L), :]
        rows.append(left(jnp.concatenate([shift, jnp.zeros((16 - NB, S), F32)], axis=0)))
        out = product(jnp.concatenate(rows, axis=0), wrot[...])
        for b in range(NB):
            pre_maps[b * L + step] = out[b * S : (b + 1) * S]
        shifts[step] = out[NB * S : NB * S + NB] + offs[pl.ds(step, NB, stride=L), :]

    advance(0, [unit] * NB, jnp.zeros((NB, S), F32))

    for step in range(1, L):
        advance(step, [pre_maps[b * L + step - 1] for b in range(NB)], shifts[step - 1])

    pad = jnp.zeros((MR - S - 1, S), F32)

    def block_map(b):
        return jnp.concatenate([pre_maps[b * L + L - 1], shifts[L - 1, b : b + 1], pad], axis=0)

    none = jnp.concatenate([unit, jnp.zeros((MR - S, S), F32)], axis=0)
    bpre[0] = none
    bpre[1] = block_map(0)
    bpre[2] = compose(block_map(0), block_map(1))
    bmaps[0] = compose(block_map(2), block_map(3))
    bmaps[1] = compose(block_map(4), block_map(5))
    bmaps[2] = compose(block_map(6), block_map(7))
    bpre[4] = compose(bpre[2], bmaps[0])
    bmaps[3] = compose(bmaps[1], bmaps[2])
    own = compose(bpre[4], bmaps[3])
    row_copy.wait_recv()
    first_slope, first_push = tangent(jnp.where(tok == 0, init[...], behind[7:8, :]), decay[0:1, :])
    own_shift = jnp.concatenate([apply_map(first_push, own, unit), jnp.zeros((MR - S - 1, S), F32)], axis=0)
    own = column(first_slope, unit) * own[:S]
    gath[z] = jnp.concatenate([own, own_shift], axis=0)
    coded[z] = encode(own, own_shift)

    def leg(r, owner):
        return pltpu.make_async_remote_copy(
            src_ref=coded.at[owner],
            dst_ref=coded.at[owner],
            send_sem=gsend.at[r],
            recv_sem=grecv.at[r],
            device_id=along_z(lax.rem(z + r, NZ)),
            device_id_type=MESH,
        )

    for r in LEGS:
        leg(r, z).start()

    for load in loads:
        load.wait()
    for q in peers:
        head_copy(q, cot, cots.at[back(q)], c_send, c_recv).wait_recv()
    hgrad[...] = jnp.zeros_like(hgrad)
    for c in range(nx):
        hgrad[...] += jnp.dot(
            jnp.concatenate([cots[2 * c], cots[2 * c + 1]], axis=1),
            w_down[pl.ds(c * 2 * S, 2 * S), :],
            preferred_element_type=F32,
        )
    for h in range(nhead):
        ctrans[pl.ds(h * S, S), :] = cots[h].astype(F32).T.astype(BF16)
    bpre[3] = compose(bpre[2], block_map(2))
    bpre[5] = compose(bpre[4], block_map(4))
    bpre[6] = compose(bpre[4], bmaps[1])
    bpre[7] = compose(bpre[6], block_map(6))
    gath[NZ] = none
    table[0] = none
    for r in (1, 7, 2, 6, 3, 5, 4):
        owner = lax.rem(z - r + NZ, NZ)
        leg(r, owner).wait_recv()
        gath[owner] = decode(coded, owner)
    pairs = [compose(gath[2 * i], gath[2 * i + 1]) for i in range(4)]
    table[1] = pairs[0]
    table[2] = pairs[2]
    low = compose(pairs[0], pairs[1])
    table[3] = low
    whole = compose(low, compose(pairs[2], pairs[3]))

    def tell_state(row):
        return pltpu.make_async_remote_copy(
            src_ref=vout,
            dst_ref=vin,
            send_sem=v_send.at[row],
            recv_sem=v_recv.at[0],
            device_id=along_y(row),
            device_id_type=MESH,
        )

    def tell_map(row, owner):
        return pltpu.make_async_remote_copy(
            src_ref=tout,
            dst_ref=tin.at[owner - 1],
            send_sem=v_send.at[row],
            recv_sem=v_recv.at[owner],
            device_id=along_y(row),
            device_id_type=MESH,
        )

    @pl.when(y == 0)
    def _():
        vout[...] = jnp.broadcast_to(apply_map(init[...], whole, unit), (8, S))
        for row in range(ny - 1, 0, -1):
            tell_state(row).start()
        vin[...] = jnp.broadcast_to(init[...], (8, S))

    for owner in range(1, ny - 1):

        @pl.when(y == owner)
        def _():
            tout[...] = encode(whole[:S], whole[S:])
            for row in range(ny - 1, owner, -1):
                tell_map(row, owner).start()

    @pl.when(y > 0)
    def _():
        tell_state(1).wait_recv()

    for owner in range(1, ny - 1):

        @pl.when(y > owner)
        def _():
            tell_map(ny - 1, owner).wait_recv()
            vin[...] = jnp.broadcast_to(apply_map(vin[0:1, :], decode(tin, owner - 1), unit), (8, S))

    v = vin[0:1, :]
    za, zb, zc = lax.div(z, 4), lax.rem(lax.div(z, 2), 2), lax.rem(z, 2)
    v = apply_map(v, table[3 * za], unit)
    v = apply_map(v, table[zb * (1 + za)], unit)
    v = apply_map(v, gath[zc * (z - 1) + (1 - zc) * NZ], unit)
    enter = column(v * first_slope + first_push, unit)

    half = S // 2

    def feat_copy(q, part, who):
        return pltpu.make_async_remote_copy(
            src_ref=feats.at[head, pl.ds(part * half, half)],
            dst_ref=feats.at[who, pl.ds(part * half, half)],
            send_sem=f_send.at[part, q[0] * 2 + q[1]],
            recv_sem=f_recv.at[part, q[0] * 2 + q[1]],
            device_id=at_head(peer(q)),
            device_id_type=MESH,
        )

    for b in range(NB):
        e = jnp.sum(enter * bpre[b, 0:S, :], axis=0, keepdims=True) + bpre[b, S : S + 1, :]
        e = jnp.broadcast_to(column(e, unit), (S, S))
        rows = [
            jnp.sum(e * pre_maps[b * L + step], axis=0, keepdims=True) + shifts[step, b : b + 1, :]
            for step in range(L)
        ]
        out = jnp.concatenate(rows, axis=0)
        states_out[b * L : (b + 1) * L, :] = out
        feats[head, b * L : (b + 1) * L, :] = out.astype(BF16)
        if b % (NB // 2) == NB // 2 - 1:
            for q in peers:
                feat_copy(q, b // (NB // 2), head).start()

    def of_chip(dx, rows):
        chip = lax.rem(x + nx - dx, nx)
        both = jnp.concatenate([feats[2 * chip, rows], feats[2 * chip + 1, rows]], axis=1)
        return both, pl.ds(pl.multiple_of(chip * 2 * S, 2 * S), 2 * S)

    ring_dx = [0, 1, nx - 1, 2]
    for part in range(2):
        rows = slice(part * half, (part + 1) * half)
        pre = jnp.zeros((half, w_up.shape[1]), F32)
        for dx in ring_dx:
            for q in ((dx, 1), (dx, 0)):
                if q != (0, 0):
                    feat_copy(q, part, back(q)).wait_recv()
            both, cols = of_chip(dx, rows)
            pre = pre + jnp.dot(both, w_up[cols, :], preferred_element_type=F32)
        gate = jax.nn.sigmoid(pre)
        hidden[rows, :] = (pre * gate).astype(BF16)
        pgrad[rows, :] = (hgrad[rows, :] * gate * (1.0 + pre * (1.0 - gate))).astype(BF16)

    rows = S * nhead // ny
    share = rows // NZ
    for i in range(ny):
        out = jnp.dot(ctrans[pl.ds(i * rows, rows), :], hidden[...], preferred_element_type=F32).astype(BF16)
        place = lax.rem(i - y + ny, ny)
        piece = sum(jnp.where(place == t, n, 0) for n, t in enumerate(TURN))
        for j in range(NZ):
            dblk[j, pl.ds(pl.multiple_of(piece * share, share), share)] = out[j * share : (j + 1) * share]
    ring_b1 = Ring(NZ, z, along_z, dblk, lb1, b1s, b1r)
    ring_b1.begin()
    for dx in ring_dx:
        both, cols = of_chip(dx, slice(0, S))
        ftrans[cols, :] = both.astype(F32).T.astype(BF16)
    for i in range(ny):
        out = jnp.dot(ftrans[pl.ds(i * rows, rows), :], pgrad[...], preferred_element_type=F32).astype(BF16)
        for j in range(NZ):
            place = lax.rem(j - z + NZ, NZ)
            piece = sum(jnp.where(place == t, n, 0) for n, t in enumerate(ORDER))
            ublk[i, pl.ds(pl.multiple_of(piece * share, share), share)] = out[j * share : (j + 1) * share]
    ring_a1 = Ring(ny, y, along_y, ublk, la1, a1s, a1r)
    ring_a1.begin()

    for h in range(nhead):
        parts[h, 0] = dot_t(hidden[...], w_down[pl.ds(h * S, S), :]).astype(BF16)
        parts[h, 1] = dot_t(pgrad[...], w_up[pl.ds(h * S, S), :]).astype(BF16)
    for q in peers:
        head_copy(q, parts.at[peer(q)], landed.at[head], o_send, o_recv).start()

    def up_copy(r):
        return pltpu.make_async_remote_copy(
            src_ref=u2blk.at[r],
            dst_ref=la2.at[r],
            send_sem=a2s.at[r],
            recv_sem=a2r.at[r],
            device_id=along_z(lax.rem(z + r, NZ)),
            device_id_type=MESH,
        )

    def up_part(c):
        out = ring_a1.total(c)
        for i in range(2):
            r = ORDER[2 * c + i]
            mine = out[i * share : (i + 1) * share]
            if r == 0:
                gup_out[...] = mine
            else:
                u2blk[r] = mine.astype(BF16)
                up_copy(r).start()

    def down_copy(r):
        return pltpu.make_async_remote_copy(
            src_ref=d2blk.at[r],
            dst_ref=lb2.at[r],
            send_sem=b2s.at[r],
            recv_sem=b2r.at[r],
            device_id=along_y(lax.rem(y + r, ny)),
            device_id_type=MESH,
        )

    def down_part(c):
        out = ring_b1.total(c)
        r = TURN[c]
        if r == 0:
            gdown_out[...] = out
        else:
            d2blk[r] = out.astype(BF16)
            down_copy(r).start()

    ring_b1.advance(0, False)
    ring_b1.advance(1, True)
    ring_a1.advance(0, False)
    ring_b1.advance(1, False)
    ring_b1.advance(2, True)
    ring_b1.advance(2, False)
    up_part(0)
    up_part(2)
    up_part(1)
    up_part(3)
    for c in (0, 2, 1, 3):
        down_part(c)
    for q in peers:
        head_copy(q, parts.at[peer(q)], landed.at[back(q)], o_send, o_recv).wait_recv()
    outs = [parts[head, i].astype(F32) for i in range(2)]
    for q in peers:
        outs = [outs[i] + landed[back(q), i].astype(F32) for i in range(2)]
    mlp_out[...] = outs[0].astype(BF16)
    sgrad_out[...] = outs[1].astype(BF16)
    for r in (1, 7, 2, 6, 3, 5, 4):
        up_copy(r).wait_recv()
        gup_out[...] += la2[r].astype(F32)
    for r in (1, 3, 2):
        down_copy(r).wait_recv()
        gdown_out[...] += lb2[r].astype(F32)

    row_copy.wait_send()
    for q in peers:
        head_copy(q, cot, cots.at[head], c_send, c_recv).wait_send()
        for part in range(2):
            feat_copy(q, part, head).wait_send()
        head_copy(q, parts.at[peer(q)], landed.at[head], o_send, o_recv).wait_send()
    for r in LEGS:
        leg(r, z).wait_send()

    @pl.when(y == 0)
    def _():
        for row in range(1, ny):
            tell_state(row).wait_send()

    for owner in range(1, ny - 1):

        @pl.when(y == owner)
        def _():
            for row in range(owner + 1, ny):
                tell_map(row, owner).wait_send()

    for ring in (ring_a1, ring_b1):
        ring.finish()
    for r in range(1, NZ):
        up_copy(r).wait_send()
    for r in range(1, ny):
        down_copy(r).wait_send()


def settle(*refs):
    for src, dst in zip(refs[:5], refs[5:]):
        dst[...] = src[...]


def on_device(ntok, nhead, guess, drive, decay, mixing, init_state, skew_gen, w_up, w_down, cotangent):
    ny = ntok // NZ
    width, ff = w_up.shape
    share = width // ntok
    vm = pl.BlockSpec(memory_space=pltpu.VMEM)
    dma = pltpu.SemaphoreType.DMA
    landing = lambda n, rows: pltpu.VMEM((2, n // 2, PIECES, rows // PIECES, ff), BF16)
    sems = lambda n: dma((2, n // 2, PIECES))
    scratch = [
        pltpu.VMEM((width, ff), BF16),
        pltpu.VMEM((width, ff), BF16),
        dma((2,)),
        pltpu.VMEM((S + 8, S), F32),
        pltpu.VMEM((8, S), F32),
        dma,
        dma,
        pltpu.VMEM((2 * S, 2 * S), BF16),
        pltpu.VMEM((S, S), F32),
        pltpu.VMEM((S, S), F32),
        pltpu.VMEM((S, S, S), F32),
        pltpu.VMEM((L, NB, S), F32),
        pltpu.VMEM((4, MR, S), F32),
        pltpu.VMEM((NB, MR, S), F32),
        pltpu.VMEM((NZ + 1, MR, S), F32),
        pltpu.VMEM((NZ, MR, S), BF16),
        dma((NZ,)),
        dma((NZ,)),
        pltpu.VMEM((4, MR, S), F32),
        pltpu.VMEM((8, S), F32),
        pltpu.VMEM((8, S), F32),
        pltpu.VMEM((ny - 2, MR, S), BF16),
        pltpu.VMEM((MR, S), BF16),
        dma((ny,)),
        dma((ny - 1,)),
        pltpu.VMEM((nhead, S, S), BF16),
        dma((2, nhead)),
        dma((2, nhead)),
        pltpu.VMEM((nhead, S, S), BF16),
        dma((nhead,)),
        dma((nhead,)),
        pltpu.VMEM((S, ff), F32),
        pltpu.VMEM((S, ff), BF16),
        pltpu.VMEM((S, ff), BF16),
        pltpu.VMEM((width, S), BF16),
        pltpu.VMEM((width, S), BF16),
        pltpu.VMEM((nhead, 2, S, S), BF16),
        pltpu.VMEM((nhead, 2, S, S), BF16),
        dma((nhead,)),
        dma((nhead,)),
        pltpu.VMEM((ny, NZ * share, ff), BF16),
        pltpu.VMEM((NZ, ny * share, ff), BF16),
        pltpu.VMEM((NZ, share, ff), BF16),
        pltpu.VMEM((ny, share, ff), BF16),
        landing(ny, NZ * share),
        pltpu.VMEM((NZ, share, ff), BF16),
        landing(NZ, ny * share),
        pltpu.VMEM((ny, share, ff), BF16),
        sems(ny),
        sems(ny),
        dma((NZ,)),
        dma((NZ,)),
        sems(NZ),
        sems(NZ),
        dma((ny,)),
        dma((ny,)),
    ]
    results = [((S, S), F32), ((S, S), BF16), ((S, S), BF16), ((share, ff), F32), ((share, ff), F32)]
    done = pl.pallas_call(
        functools.partial(kernel, ntok, nhead),
        out_shape=tuple(pltpu.VMEM(*r) for r in results),
        in_specs=[vm] * 6 + [pl.BlockSpec(memory_space=pl.ANY)] * 2 + [vm],
        out_specs=[vm] * 5,
        scratch_shapes=scratch,
        compiler_params=pltpu.CompilerParams(
            collective_id=0, has_side_effects=True, vmem_limit_bytes=56 * 1024 * 1024
        ),
    )(
        guess,
        drive,
        decay,
        mixing.reshape(1, S),
        init_state.reshape(1, S),
        skew_gen.reshape(S, S),
        w_up,
        w_down,
        cotangent,
    )
    return pl.pallas_call(
        settle,
        out_shape=tuple(jax.ShapeDtypeStruct(*r) for r in results),
        in_specs=[vm] * 5,
        out_specs=[vm] * 5,
    )(*[pltpu.with_memory_space_constraint(d, pltpu.VMEM) for d in done])


def solution(mesh):
    placed = (
        P("tok", "head"),
        P("tok", "head"),
        P("tok", "head"),
        P("head"),
        P("head"),
        P("head", None, None),
        P(None, "head"),
        P(None, "head"),
        P("tok", "head"),
    )
    return jax.shard_map(
        functools.partial(on_device, mesh.shape["tok"], mesh.shape["head"]),
        mesh=mesh,
        in_specs=placed,
        out_specs=(P("tok", "head"),) * 5,
        check_vma=False,
    )
```

```python
import functools

import jax
import jax.numpy as jnp
from jax import lax
from jax.experimental import pallas as pl
from jax.experimental.pallas import tpu as pltpu
from jax.sharding import PartitionSpec as P

MESH = pl.DeviceIdType.MESH
F32, BF16 = jnp.float32, jnp.bfloat16
S = 128
NZ = 8
NB, L = 8, 16
MR = 144
SPREAD = 86.0
NEWTON = 11
LEGS = (4, 3, 5, 2, 6, 1, 7)
PIECES = 4
ORDER = (4, 3, 6, 1, 5, 2, 7, 0)
TURN = (2, 3, 1, 0)


def split(x):
    hi = x.astype(BF16)
    return hi, (x - hi.astype(F32)).astype(BF16)


def left(x):
    return jnp.concatenate(split(x), axis=1)


def right(x):
    both = jnp.concatenate(split(x), axis=1)
    return jnp.concatenate([both, both], axis=0)


def product(l, r):
    out = jnp.dot(l, r, preferred_element_type=F32)
    return out[:, :S] + out[:, S:]


def mm(a, b):
    return product(left(a), right(b))


def compose(first, then):
    out = mm(first, then[:S])
    return jnp.concatenate([out[:S], out[S:] + then[S:]], axis=0)


def eye():
    rows = lax.broadcasted_iota(jnp.int32, (S, S), 0)
    cols = lax.broadcasted_iota(jnp.int32, (S, S), 1)
    return jnp.where(rows == cols, 1.0, 0.0).astype(F32)


def column(v, unit):
    return jnp.sum(unit * v, axis=1, keepdims=True)


def apply_map(v, m, unit):
    return jnp.sum(column(v, unit) * m[:S], axis=0, keepdims=True) + m[S : S + 1]


def dot_t(a, b):
    return lax.dot_general(a, b, (((1,), (1,)), ((), ())), preferred_element_type=F32)


def encode(matrix, shift):
    high, rest = split(shift)
    low = (shift - high.astype(F32) - rest.astype(F32)).astype(BF16)
    rows = [high[:1], rest[:1], low[:1], high[1:14]]
    matrix = jnp.exp(jnp.clip(matrix, -1.01, 1.01) * SPREAD).astype(BF16)
    return jnp.concatenate([matrix, jnp.concatenate([r.astype(F32) for r in rows], axis=0).astype(BF16)], axis=0)


def decode(ref, at):
    matrix = jnp.log(ref[at, 0:S, :].astype(F32)) * (1.0 / SPREAD)
    tail = ref[at, S:MR, :].astype(F32)
    shift = tail[0:1] + tail[1:2] + tail[2:3]
    return jnp.concatenate([matrix, shift, jnp.zeros((MR - S - 1, S), F32)], axis=0)


class Ring:
    def __init__(self, n, me, device, blocks, landing, send, recv):
        self.n, self.me, self.device = n, me, device
        self.blocks, self.landing, self.send, self.recv = blocks, landing, send, recv
        self.rows = blocks.shape[1] // PIECES

    def owner(self, d, hop):
        way = 1 if d == 0 else -1
        return lax.rem(self.me + way * (self.n // 2 - hop) + 2 * self.n, self.n)

    def at(self, c):
        return pl.ds(c * self.rows, self.rows)

    def copy(self, d, hop, c):
        target = lax.rem(self.me + (1 if d == 0 else -1) + self.n, self.n)
        return pltpu.make_async_remote_copy(
            src_ref=self.blocks.at[self.owner(d, hop), self.at(c)],
            dst_ref=self.landing.at[d, hop, c],
            send_sem=self.send.at[d, hop, c],
            recv_sem=self.recv.at[d, hop, c],
            device_id=self.device(target),
            device_id_type=MESH,
        )

    @staticmethod
    def first(d):
        return (0, 1) if d == 0 else (2, 3)

    def begin(self):
        for i in range(2):
            for d in range(2):
                self.copy(d, 0, self.first(d)[i]).start()
        for i in range(2):
            for d in range(2):
                self.copy(d, 1, self.first(1 - d)[i]).start()

    def advance(self, hop, early):
        for i in range(2):
            for d in range(2):
                c = self.first(1 - d if early else d)[i]
                self.copy(d, hop, c).wait_recv()
                to = self.owner(d, hop + 1)
                self.blocks[to, self.at(c)] = (
                    self.blocks[to, self.at(c)].astype(F32) + self.landing[d, hop, c].astype(F32)
                ).astype(BF16)
                self.copy(d, hop + 1, c).start()

    def total(self, c):
        last = self.n // 2 - 1
        out = self.blocks[self.me, self.at(c)].astype(F32)
        for d in range(2):
            self.copy(d, last, c).wait_recv()
            out = out + self.landing[d, last, c].astype(F32)
        return out

    def finish(self):
        for hop in range(self.n // 2):
            for d in range(2):
                for c in self.first(d) if hop == 0 else range(PIECES):
                    self.copy(d, hop, c).wait_send()


def kernel(
    ntok,
    nhead,
    guess,
    drive,
    decay,
    mixing,
    init,
    skew,
    w_up_hbm,
    w_down_hbm,
    cot,
    states_out,
    mlp_out,
    sgrad_out,
    gup_out,
    gdown_out,
    w_up,
    w_down,
    w_sem,
    shifted,
    behind,
    row_send,
    row_recv,
    rot,
    wrot,
    slopes,
    offs,
    pre_maps,
    shifts,
    bmaps,
    bpre,
    gath,
    coded,
    gsend,
    grecv,
    table,
    vin,
    vout,
    tin,
    tout,
    v_send,
    v_recv,
    feats,
    f_send,
    f_recv,
    cots,
    c_send,
    c_recv,
    hgrad,
    hidden,
    pgrad,
    ftrans,
    ctrans,
    parts,
    landed,
    o_send,
    o_recv,
    ublk,
    dblk,
    u2blk,
    d2blk,
    la1,
    la2,
    lb1,
    lb2,
    a1s,
    a1r,
    a2s,
    a2r,
    b1s,
    b1r,
    b2s,
    b2r,
):
    ny, nx = ntok // NZ, nhead // 2
    tok, head = lax.axis_index("tok"), lax.axis_index("head")
    y, z = lax.div(tok, NZ), lax.rem(tok, NZ)
    x, core = lax.div(head, 2), lax.rem(head, 2)

    def along_z(target):
        return {"tok": y * NZ + target, "head": head}

    def along_y(target):
        return {"tok": target * NZ + z, "head": head}

    def at_tok(target):
        return {"tok": target, "head": head}

    def at_head(target):
        return {"tok": tok, "head": target}

    peers = [(dx, flip) for dx in ([0, 1, nx - 1, 2] if nx >= 4 else range(nx)) for flip in (1, 0)]
    peers = [q for q in peers if q != (0, 0)]

    def peer(q):
        return lax.rem(x + q[0], nx) * 2 + lax.rem(core + q[1], 2)

    after, before_me = lax.rem(tok + 1, ntok), lax.rem(tok + ntok - 1, ntok)

    barrier = pltpu.get_barrier_semaphore()
    greet = [along_z(lax.rem(z + i, NZ)) for i in range(1, NZ)]
    greet += [along_y(lax.rem(y + i, ny)) for i in range(1, ny)]
    greet += [at_tok(after), at_tok(before_me)]
    greet += [at_head(peer(q)) for q in peers]
    for who in greet:
        pl.semaphore_signal(barrier, inc=1, device_id=who, device_id_type=MESH)
    loads = [
        pltpu.make_async_copy(w_up_hbm, w_up, w_sem.at[0]),
        pltpu.make_async_copy(w_down_hbm, w_down, w_sem.at[1]),
    ]
    for load in loads:
        load.start()

    unit = eye()
    k = skew[...]
    a = unit + k
    kk = mm(k, k)
    bound = jnp.sqrt(jnp.sum(jnp.sum(kk * kk, axis=1, keepdims=True), axis=0, keepdims=True) * 0.5)
    top = 1.0 + 1.01 * bound
    scale = 2.0 / (1.0 + top)
    gap = (top - 1.0) / (top + 1.0)

    def newton(v, t, gap):
        square = gap * gap
        wide = 2.0 / (2.0 - square)
        out = product(left(jnp.concatenate([t, v], axis=0)), right(wide * (2.0 * unit - t)))
        return out[S:], out[:S], square / (2.0 - square)

    v, t = (unit - k) * scale, (unit - kk) * scale
    for _ in range(NEWTON):
        v, t, gap = newton(v, t, gap)
    t = jnp.dot(a, v, precision=lax.Precision.HIGHEST, preferred_element_type=F32)
    v = v + mm(v, unit - t)
    rot_t = 2.0 * v - unit
    rot[...] = rot_t
    wrot[...] = right(rot_t)

    pl.semaphore_wait(barrier, len(greet))
    row_copy = pltpu.make_async_remote_copy(
        src_ref=guess.at[pl.ds(S - 8, 8)],
        dst_ref=behind,
        send_sem=row_send,
        recv_sem=row_recv,
        device_id=at_tok(after),
        device_id_type=MESH,
    )
    row_copy.start()

    def head_copy(q, src, dst, send, recv):
        return pltpu.make_async_remote_copy(
            src_ref=src,
            dst_ref=dst,
            send_sem=send.at[q[0] * 2 + q[1]],
            recv_sem=recv.at[q[0] * 2 + q[1]],
            device_id=at_head(peer(q)),
            device_id_type=MESH,
        )

    def back(q):
        return lax.rem(x + nx - q[0], nx) * 2 + lax.rem(core + q[1], 2)

    for q in peers:
        head_copy(q, cot, cots.at[head], c_send, c_recv).start()
    cots[head] = cot[...]

    m = mixing[...]

    def tangent(before, decay):
        bent = jnp.tanh(before)
        curve = 1.0 - bent * bent
        return (1.0 - m) * decay + m * curve, m * (bent - curve * before)

    shifted[pl.ds(8, S), :] = guess[...]
    first = lax.broadcasted_iota(jnp.int32, (S, S), 0) == 0
    slope, push = tangent(jnp.where(first, 0.0, shifted[pl.ds(7, S), :]), decay[...])
    slopes[...] = jnp.where(first, 1.0, slope)
    offs[...] = product(left(jnp.where(first, 0.0, push)), wrot[...]) + drive[...]

    def advance(step, blocks, shift):
        rows = [left(blocks[b] * slopes[pl.ds(b * L + step, 1), :]) for b in range(NB)]
        shift = shift * slopes[pl.ds(step, NB, stride=L), :]
        rows.append(left(jnp.concatenate([shift, jnp.zeros((16 - NB, S), F32)], axis=0)))
        out = product(jnp.concatenate(rows, axis=0), wrot[...])
        for b in range(NB):
            pre_maps[b * L + step] = out[b * S : (b + 1) * S]
        shifts[step] = out[NB * S : NB * S + NB] + offs[pl.ds(step, NB, stride=L), :]

    pre_maps[0] = rot[...]
    for b in range(1, NB):
        pre_maps[b * L] = column(slopes[b * L : b * L + 1, :], unit) * rot[...]
    shifts[0] = offs[pl.ds(0, NB, stride=L), :]

    for step in range(1, L):
        advance(step, [pre_maps[b * L + step - 1] for b in range(NB)], shifts[step - 1])

    pad = jnp.zeros((MR - S - 1, S), F32)

    def block_map(b):
        return jnp.concatenate([pre_maps[b * L + L - 1], shifts[L - 1, b : b + 1], pad], axis=0)

    none = jnp.concatenate([unit, jnp.zeros((MR - S, S), F32)], axis=0)
    bpre[0] = none
    bpre[1] = block_map(0)
    bpre[2] = compose(block_map(0), block_map(1))
    bmaps[0] = compose(block_map(2), block_map(3))
    bmaps[1] = compose(block_map(4), block_map(5))
    bmaps[2] = compose(block_map(6), block_map(7))
    bpre[4] = compose(bpre[2], bmaps[0])
    bmaps[3] = compose(bmaps[1], bmaps[2])
    own = compose(bpre[4], bmaps[3])
    row_copy.wait_recv()
    first_slope, first_push = tangent(jnp.where(tok == 0, init[...], behind[7:8, :]), decay[0:1, :])
    own_shift = jnp.concatenate([apply_map(first_push, own, unit), jnp.zeros((MR - S - 1, S), F32)], axis=0)
    own = column(first_slope, unit) * own[:S]
    gath[z] = jnp.concatenate([own, own_shift], axis=0)
    coded[z] = encode(own, own_shift)

    def leg(r, owner):
        return pltpu.make_async_remote_copy(
            src_ref=coded.at[owner],
            dst_ref=coded.at[owner],
            send_sem=gsend.at[r],
            recv_sem=grecv.at[r],
            device_id=along_z(lax.rem(z + r, NZ)),
            device_id_type=MESH,
        )

    for r in LEGS:
        leg(r, z).start()

    for load in loads:
        load.wait()
    for q in peers:
        head_copy(q, cot, cots.at[back(q)], c_send, c_recv).wait_recv()
    hgrad[...] = jnp.zeros_like(hgrad)
    for c in range(nx):
        hgrad[...] += jnp.dot(
            jnp.concatenate([cots[2 * c], cots[2 * c + 1]], axis=1),
            w_down[pl.ds(c * 2 * S, 2 * S), :],
            preferred_element_type=F32,
        )
    for h in range(nhead):
        ctrans[pl.ds(h * S, S), :] = cots[h].astype(F32).T.astype(BF16)
    bpre[3] = compose(bpre[2], block_map(2))
    bpre[5] = compose(bpre[4], block_map(4))
    bpre[6] = compose(bpre[4], bmaps[1])
    bpre[7] = compose(bpre[6], block_map(6))
    gath[NZ] = none
    table[0] = none
    for r in LEGS:
        owner = lax.rem(z - r + NZ, NZ)
        leg(r, owner).wait_recv()
        gath[owner] = decode(coded, owner)
    pairs = [compose(gath[2 * i], gath[2 * i + 1]) for i in range(4)]
    table[1] = pairs[0]
    table[2] = pairs[2]
    low = compose(pairs[0], pairs[1])
    table[3] = low
    whole = compose(low, compose(pairs[2], pairs[3]))

    def tell_state(row):
        return pltpu.make_async_remote_copy(
            src_ref=vout,
            dst_ref=vin,
            send_sem=v_send.at[row],
            recv_sem=v_recv.at[0],
            device_id=along_y(row),
            device_id_type=MESH,
        )

    def tell_map(row, owner):
        return pltpu.make_async_remote_copy(
            src_ref=tout,
            dst_ref=tin.at[owner - 1],
            send_sem=v_send.at[row],
            recv_sem=v_recv.at[owner],
            device_id=along_y(row),
            device_id_type=MESH,
        )

    @pl.when(y == 0)
    def _():
        vout[...] = jnp.broadcast_to(apply_map(init[...], whole, unit), (8, S))
        for row in range(ny - 1, 0, -1):
            tell_state(row).start()
        vin[...] = jnp.broadcast_to(init[...], (8, S))

    for owner in range(1, ny - 1):

        @pl.when(y == owner)
        def _():
            tout[...] = encode(whole[:S], whole[S:])
            for row in range(ny - 1, owner, -1):
                tell_map(row, owner).start()

    @pl.when(y > 0)
    def _():
        tell_state(1).wait_recv()

    for owner in range(1, ny - 1):

        @pl.when(y > owner)
        def _():
            tell_map(ny - 1, owner).wait_recv()
            vin[...] = jnp.broadcast_to(apply_map(vin[0:1, :], decode(tin, owner - 1), unit), (8, S))

    v = vin[0:1, :]
    za, zb, zc = lax.div(z, 4), lax.rem(lax.div(z, 2), 2), lax.rem(z, 2)
    v = apply_map(v, table[3 * za], unit)
    v = apply_map(v, table[zb * (1 + za)], unit)
    v = apply_map(v, gath[zc * (z - 1) + (1 - zc) * NZ], unit)
    enter = column(v * first_slope + first_push, unit)

    half = S // 2

    def feat_copy(q, part, who):
        return pltpu.make_async_remote_copy(
            src_ref=feats.at[head, pl.ds(part * half, half)],
            dst_ref=feats.at[who, pl.ds(part * half, half)],
            send_sem=f_send.at[part, q[0] * 2 + q[1]],
            recv_sem=f_recv.at[part, q[0] * 2 + q[1]],
            device_id=at_head(peer(q)),
            device_id_type=MESH,
        )

    for b in range(NB):
        e = jnp.sum(enter * bpre[b, 0:S, :], axis=0, keepdims=True) + bpre[b, S : S + 1, :]
        e = jnp.broadcast_to(column(e, unit), (S, S))
        rows = [
            jnp.sum(e * pre_maps[b * L + step], axis=0, keepdims=True) + shifts[step, b : b + 1, :]
            for step in range(L)
        ]
        out = jnp.concatenate(rows, axis=0)
        states_out[b * L : (b + 1) * L, :] = out
        feats[head, b * L : (b + 1) * L, :] = out.astype(BF16)
        if b % (NB // 2) == NB // 2 - 1:
            for q in peers[-2:] + peers[1:-2] + peers[:1]:
                feat_copy(q, b // (NB // 2), head).start()

    def of_chip(dx, rows):
        chip = lax.rem(x + nx - dx, nx)
        both = jnp.concatenate([feats[2 * chip, rows], feats[2 * chip + 1, rows]], axis=1)
        return both, pl.ds(pl.multiple_of(chip * 2 * S, 2 * S), 2 * S)

    ring_dx = [0, 1, nx - 1, 2]
    for part in range(2):
        rows = slice(part * half, (part + 1) * half)
        pre = jnp.zeros((half, w_up.shape[1]), F32)
        for dx in ring_dx:
            for q in ((dx, 1), (dx, 0)):
                if q != (0, 0):
                    feat_copy(q, part, back(q)).wait_recv()
            both, cols = of_chip(dx, rows)
            pre = pre + jnp.dot(both, w_up[cols, :], preferred_element_type=F32)
        gate = jax.nn.sigmoid(pre)
        hidden[rows, :] = (pre * gate).astype(BF16)
        pgrad[rows, :] = (hgrad[rows, :] * gate * (1.0 + pre * (1.0 - gate))).astype(BF16)

    rows = S * nhead // ny
    share = rows // NZ
    for i in range(ny):
        out = jnp.dot(ctrans[pl.ds(i * rows, rows), :], hidden[...], preferred_element_type=F32).astype(BF16)
        place = lax.rem(i - y + ny, ny)
        piece = sum(jnp.where(place == t, n, 0) for n, t in enumerate(TURN))
        for j in range(NZ):
            dblk[j, pl.ds(pl.multiple_of(piece * share, share), share)] = out[j * share : (j + 1) * share]
    ring_b1 = Ring(NZ, z, along_z, dblk, lb1, b1s, b1r)
    ring_b1.begin()
    for dx in ring_dx:
        both, cols = of_chip(dx, slice(0, S))
        ftrans[cols, :] = both.astype(F32).T.astype(BF16)
    for i in range(ny):
        out = jnp.dot(ftrans[pl.ds(i * rows, rows), :], pgrad[...], preferred_element_type=F32).astype(BF16)
        for j in range(NZ):
            place = lax.rem(j - z + NZ, NZ)
            piece = sum(jnp.where(place == t, n, 0) for n, t in enumerate(ORDER))
            ublk[i, pl.ds(pl.multiple_of(piece * share, share), share)] = out[j * share : (j + 1) * share]
    ring_a1 = Ring(ny, y, along_y, ublk, la1, a1s, a1r)
    ring_a1.begin()

    for h in range(nhead):
        parts[h, 0] = dot_t(hidden[...], w_down[pl.ds(h * S, S), :]).astype(BF16)
        parts[h, 1] = dot_t(pgrad[...], w_up[pl.ds(h * S, S), :]).astype(BF16)
    for q in peers:
        head_copy(q, parts.at[peer(q)], landed.at[head], o_send, o_recv).start()

    def up_copy(r):
        return pltpu.make_async_remote_copy(
            src_ref=u2blk.at[r],
            dst_ref=la2.at[r],
            send_sem=a2s.at[r],
            recv_sem=a2r.at[r],
            device_id=along_z(lax.rem(z + r, NZ)),
            device_id_type=MESH,
        )

    def up_part(c):
        out = ring_a1.total(c)
        for i in range(2):
            r = ORDER[2 * c + i]
            mine = out[i * share : (i + 1) * share]
            if r == 0:
                gup_out[...] = mine
            else:
                u2blk[r] = mine.astype(BF16)
                up_copy(r).start()

    def down_copy(r):
        return pltpu.make_async_remote_copy(
            src_ref=d2blk.at[r],
            dst_ref=lb2.at[r],
            send_sem=b2s.at[r],
            recv_sem=b2r.at[r],
            device_id=along_y(lax.rem(y + r, ny)),
            device_id_type=MESH,
        )

    def down_part(c):
        out = ring_b1.total(c)
        r = TURN[c]
        if r == 0:
            gdown_out[...] = out
        else:
            d2blk[r] = out.astype(BF16)
            down_copy(r).start()

    ring_b1.advance(0, False)
    ring_b1.advance(1, True)
    ring_a1.advance(0, False)
    ring_b1.advance(1, False)
    ring_b1.advance(2, True)
    ring_b1.advance(2, False)
    up_part(0)
    up_part(2)
    up_part(1)
    up_part(3)
    for c in (0, 2, 1, 3):
        down_part(c)
    for q in peers:
        head_copy(q, parts.at[peer(q)], landed.at[back(q)], o_send, o_recv).wait_recv()
    outs = [parts[head, i].astype(F32) for i in range(2)]
    for q in peers:
        outs = [outs[i] + landed[back(q), i].astype(F32) for i in range(2)]
    mlp_out[...] = outs[0].astype(BF16)
    sgrad_out[...] = outs[1].astype(BF16)
    for r in (1, 7, 2, 6, 3, 5, 4):
        up_copy(r).wait_recv()
        gup_out[...] += la2[r].astype(F32)
    for r in (1, 3, 2):
        down_copy(r).wait_recv()
        gdown_out[...] += lb2[r].astype(F32)

    row_copy.wait_send()
    for q in peers:
        head_copy(q, cot, cots.at[head], c_send, c_recv).wait_send()
        for part in range(2):
            feat_copy(q, part, head).wait_send()
        head_copy(q, parts.at[peer(q)], landed.at[head], o_send, o_recv).wait_send()
    for r in LEGS:
        leg(r, z).wait_send()

    @pl.when(y == 0)
    def _():
        for row in range(1, ny):
            tell_state(row).wait_send()

    for owner in range(1, ny - 1):

        @pl.when(y == owner)
        def _():
            for row in range(owner + 1, ny):
                tell_map(row, owner).wait_send()

    for ring in (ring_a1, ring_b1):
        ring.finish()
    for r in range(1, NZ):
        up_copy(r).wait_send()
    for r in range(1, ny):
        down_copy(r).wait_send()


def settle(*refs):
    for src, dst in zip(refs[:5], refs[5:]):
        dst[...] = src[...]


def on_device(ntok, nhead, guess, drive, decay, mixing, init_state, skew_gen, w_up, w_down, cotangent):
    ny = ntok // NZ
    width, ff = w_up.shape
    share = width // ntok
    vm = pl.BlockSpec(memory_space=pltpu.VMEM)
    dma = pltpu.SemaphoreType.DMA
    landing = lambda n, rows: pltpu.VMEM((2, n // 2, PIECES, rows // PIECES, ff), BF16)
    sems = lambda n: dma((2, n // 2, PIECES))
    scratch = [
        pltpu.VMEM((width, ff), BF16),
        pltpu.VMEM((width, ff), BF16),
        dma((2,)),
        pltpu.VMEM((S + 8, S), F32),
        pltpu.VMEM((8, S), F32),
        dma,
        dma,
        pltpu.VMEM((S, S), F32),
        pltpu.VMEM((2 * S, 2 * S), BF16),
        pltpu.VMEM((S, S), F32),
        pltpu.VMEM((S, S), F32),
        pltpu.VMEM((S, S, S), F32),
        pltpu.VMEM((L, NB, S), F32),
        pltpu.VMEM((4, MR, S), F32),
        pltpu.VMEM((NB, MR, S), F32),
        pltpu.VMEM((NZ + 1, MR, S), F32),
        pltpu.VMEM((NZ, MR, S), BF16),
        dma((NZ,)),
        dma((NZ,)),
        pltpu.VMEM((4, MR, S), F32),
        pltpu.VMEM((8, S), F32),
        pltpu.VMEM((8, S), F32),
        pltpu.VMEM((ny - 2, MR, S), BF16),
        pltpu.VMEM((MR, S), BF16),
        dma((ny,)),
        dma((ny - 1,)),
        pltpu.VMEM((nhead, S, S), BF16),
        dma((2, nhead)),
        dma((2, nhead)),
        pltpu.VMEM((nhead, S, S), BF16),
        dma((nhead,)),
        dma((nhead,)),
        pltpu.VMEM((S, ff), F32),
        pltpu.VMEM((S, ff), BF16),
        pltpu.VMEM((S, ff), BF16),
        pltpu.VMEM((width, S), BF16),
        pltpu.VMEM((width, S), BF16),
        pltpu.VMEM((nhead, 2, S, S), BF16),
        pltpu.VMEM((nhead, 2, S, S), BF16),
        dma((nhead,)),
        dma((nhead,)),
        pltpu.VMEM((ny, NZ * share, ff), BF16),
        pltpu.VMEM((NZ, ny * share, ff), BF16),
        pltpu.VMEM((NZ, share, ff), BF16),
        pltpu.VMEM((ny, share, ff), BF16),
        landing(ny, NZ * share),
        pltpu.VMEM((NZ, share, ff), BF16),
        landing(NZ, ny * share),
        pltpu.VMEM((ny, share, ff), BF16),
        sems(ny),
        sems(ny),
        dma((NZ,)),
        dma((NZ,)),
        sems(NZ),
        sems(NZ),
        dma((ny,)),
        dma((ny,)),
    ]
    results = [((S, S), F32), ((S, S), BF16), ((S, S), BF16), ((share, ff), F32), ((share, ff), F32)]
    done = pl.pallas_call(
        functools.partial(kernel, ntok, nhead),
        out_shape=tuple(pltpu.VMEM(*r) for r in results),
        in_specs=[vm] * 6 + [pl.BlockSpec(memory_space=pl.ANY)] * 2 + [vm],
        out_specs=[vm] * 5,
        scratch_shapes=scratch,
        compiler_params=pltpu.CompilerParams(
            collective_id=0, has_side_effects=True, vmem_limit_bytes=56 * 1024 * 1024
        ),
    )(
        guess,
        drive,
        decay,
        mixing.reshape(1, S),
        init_state.reshape(1, S),
        skew_gen.reshape(S, S),
        w_up,
        w_down,
        cotangent,
    )
    return pl.pallas_call(
        settle,
        out_shape=tuple(jax.ShapeDtypeStruct(*r) for r in results),
        in_specs=[vm] * 5,
        out_specs=[vm] * 5,
    )(*[pltpu.with_memory_space_constraint(d, pltpu.VMEM) for d in done])


def solution(mesh):
    placed = (
        P("tok", "head"),
        P("tok", "head"),
        P("tok", "head"),
        P("head"),
        P("head"),
        P("head", None, None),
        P(None, "head"),
        P(None, "head"),
        P("tok", "head"),
    )
    return jax.shard_map(
        functools.partial(on_device, mesh.shape["tok"], mesh.shape["head"]),
        mesh=mesh,
        in_specs=placed,
        out_specs=(P("tok", "head"),) * 5,
        check_vma=False,
    )
```
